32 devices in a mesh: space: 8 (over z, core), chan: 4 (over y, x).
Axes of the slice: x: 2, y: 2, z: 4, core: 2. Of those that a mesh axis runs over, the one named last changes fastest.
Arguments:
- tensor_field: bfloat16 [16, 512, 4096], P('space', 'chan'), may hold values from -6 to 6
- radial: bfloat16 [5, 4, 128, 128], replicated, may hold values from -0.078125 to 0.078125
Outputs:
- convolved: bfloat16 [16, 512, 4096], P('space', 'chan')
The draws below stay inside these ranges and needn't reach their ends.
All inputs are finite; a program needn't handle non-finite values.
Results may differ from the reference program's by a relative error of at most 0.006.
Values may be sent and summed in bfloat16 or wider, within the bound.
No kernel may reach another device: no remote copies, remote signals or barrier semaphores. Data moves between devices by JAX's collectives and lax.ppermute only.
A program may use at most 192 MiB of HBM per device.

```python
import jax
import jax.numpy as jnp
import numpy as np
from jax import lax

CS = 128
C = 512
NX = 64
NY = 64
NZ = 16


def block_scale(rng, dims, split, smallest, largest):
    def one(dim, blocks):
        steps = jax.random.uniform(jax.random.fold_in(jax.random.fold_in(rng, 6), dim), (blocks,), jnp.float32, smallest / len(split), largest / len(split))
        return jnp.repeat(jnp.exp(steps), dims[dim] // blocks).reshape((-1,) + (1,) * (len(dims) - dim - 1))

    gain = one(*split[0])
    for cut in split[1:]:
        gain = gain * one(*cut)
    return gain


def centred(rng, extent, scale, reach, pieces=(), kind=jnp.bfloat16):
    entries = jax.random.normal(rng, extent, jnp.float32) * scale
    if len(pieces) > 0:
        entries = block_scale(rng, extent, pieces, -0.22, 0.18) * entries
    return jnp.clip(entries, min=-reach, max=reach).astype(kind)


def setup_inputs(seed: int = 0) -> dict:
    keys = jax.random.split(jax.random.key(seed), 3)
    return {
        "tensor_field": centred(keys[0], (NZ, C, NY * NX), 1.0, 6.0, ((0, 8), (1, 4))),
        "radial": centred(keys[1], (5, 4, CS, CS), (54 * CS) ** -0.5, 0.078125),
    }


def offset_table():
    listed = []
    for step_depth in (-1, 0, 1):
        for step_row in (-1, 0, 1):
            for step_col in (-1, 0, 1):
                listed.append((step_depth, step_row, step_col))
    return np.array(listed, dtype=np.int64)

def kernel_table(radial):
    offsets = offset_table()
    shells = np.abs(offsets).sum(axis=1)
    scaled = offsets / np.sqrt(np.maximum(shells, 1))[:, None]
    direction = jnp.asarray(scaled, dtype=jnp.float32)
    weights = radial.astype(jnp.float32)[:, shells]
    units = [direction[:, 2][:, None, None], direction[:, 1][:, None, None], direction[:, 0][:, None, None]]
    scalar_w = weights[0]
    vector_w = weights[1]
    lift_w = weights[2]
    project_w = weights[3]
    tensor_w = weights[4]
    scalar_rows = jnp.concatenate([scalar_w] + [unit * lift_w for unit in units], axis=2)
    row_sets = [scalar_rows]
    for first in range(3):
        blocks = [units[first] * project_w]
        for second in range(3):
            block = units[first] * units[second] * tensor_w
            if first == second:
                block = block + vector_w
            blocks.append(block)
        row_sets.append(jnp.concatenate(blocks, axis=2))
    kernels = jnp.concatenate(row_sets, axis=1)
    return kernels.astype(jnp.bfloat16)

def reference(tensor_field, radial):
    components = 4 * CS
    kernels = kernel_table(radial).astype(jnp.float32).reshape(3, 9, components, components)
    depth_count = tensor_field.shape[0]

    def one_plane(plane_index):
        neighbours = jnp.stack([lax.dynamic_index_in_dim(tensor_field, ((plane_index + step_depth) % depth_count).astype(jnp.int32), 0, keepdims=False) for step_depth in (-1, 0, 1)]).astype(jnp.float32)
        lattice = neighbours.reshape(3, components, NY, NX)
        shifted = jnp.stack([jnp.roll(lattice, (-step_row, -step_col), axis=(2, 3)) for step_row in (-1, 0, 1) for step_col in (-1, 0, 1)], axis=1)
        shifted = shifted.reshape(3, 9, components, NY * NX)
        return jnp.einsum('abio,abip->op', kernels, shifted, precision=lax.Precision.HIGHEST).astype(jnp.bfloat16)
    return lax.map(one_plane, jnp.arange(depth_count, dtype=jnp.int32))
```

```python
import functools

import jax
import jax.numpy as jnp
import numpy as np
from jax import lax
from jax.experimental import pallas as pl
from jax.experimental.pallas import tpu as pltpu
from jax.sharding import PartitionSpec as P


CS = 128
LANES = 128
HALF = 2048
SLAB = HALF + LANES
CHUNK = 512


def weight_tables():
    index = np.zeros((8, 4, 8, 2), np.int32)
    scale = np.zeros((8, 4, 8, 2), np.float32)
    for comp in range(4):
        for odd in range(2):
            gathered = comp ^ (2 if odd else 1)
            reduced = comp ^ (1 if odd else 2)
            pairs = [(comp, comp), (comp, reduced), (gathered, reduced), (gathered, comp)]
            for slot, (i, o) in enumerate(pairs):
                z_odd = (i == 3) != (o == 3)
                for t in range(2):
                    for f in range(4):
                        if z_odd and f >= 2:
                            continue
                        d = (t, f % 2, 1 if (z_odd or f >= 2) else 0)
                        s = sum(d)
                        u = np.float32(np.array(d) / np.sqrt(max(s, 1)))
                        sign = np.float32(-1.0 if (z_odd and odd) else 1.0)
                        kind, first, second = 0, np.float32(0.0), np.float32(0.0)
                        if i == 0 and o == 0:
                            kind, first = 0, np.float32(1.0)
                        elif i == 0:
                            kind, first = 2, u[o - 1]
                        elif o == 0:
                            kind, first = 3, u[i - 1]
                        else:
                            kind = 1
                            first = np.float32(1.0 if i == o else 0.0)
                            second = u[i - 1] * u[o - 1]
                        index[comp * 2 + odd, slot, t * 4 + f] = (kind * 4 + s, 16 + s)
                        scale[comp * 2 + odd, slot, t * 4 + f] = (sign * first, sign * second)
    return index.reshape(8, 64), scale.reshape(8, 64)


def weights_kernel(role_ref, index_ref, scale_ref, radial_ref, out_ref):
    role = role_ref[0]
    for slot in range(4):
        for t in range(2):
            for f in range(4):
                at = (slot * 8 + t * 4 + f) * 2
                first = radial_ref[index_ref[role, at]].astype(jnp.float32) * scale_ref[role, at]
                second = radial_ref[index_ref[role, at + 1]].astype(jnp.float32) * scale_ref[role, at + 1]
                block = jnp.transpose(first + second).astype(jnp.bfloat16)
                out_ref[slot, t * CS : (t + 1) * CS, f * CS : (f + 1) * CS] = block


def weights(role, radial):
    index, scale = weight_tables()
    smem = pl.BlockSpec(memory_space=pltpu.SMEM)
    vmem = pl.BlockSpec(memory_space=pltpu.VMEM)
    return pl.pallas_call(
        weights_kernel,
        out_shape=jax.ShapeDtypeStruct((4, 2 * CS, 4 * CS), jnp.bfloat16),
        in_specs=[smem, smem, smem, vmem],
        out_specs=vmem,
        cost_estimate=pl.CostEstimate(flops=0, bytes_accessed=4 << 20, transcendentals=0),
        name="weights",
    )(role, jnp.asarray(index), jnp.asarray(scale), radial.reshape(20, CS, CS))


def slab_kernel(role_ref, field_ref, keep_ref, give_ref):
    odd = role_ref[0] % 2
    low = lax.broadcasted_iota(jnp.int32, (field_ref.shape[1], LANES), 1) < LANES // 2
    parts = []
    for half in range(2):
        start = half * HALF
        after = field_ref[0, :, (start + HALF) % (2 * HALF) : (start + HALF) % (2 * HALF) + LANES]
        before = field_ref[0, :, (start - LANES) % (2 * HALF) : (start - LANES) % (2 * HALF) + LANES]
        parts.append((field_ref[0, :, start : start + HALF], jnp.where(low, after, before)))
    for parity in range(2):

        @pl.when(odd == parity)
        def _():
            for ref, half in ((keep_ref, parity), (give_ref, 1 - parity)):
                ref[0, :, :HALF] = parts[half][0]
                ref[0, :, HALF:] = parts[half][1]


def slabs(role, field):
    rows = 32
    slab = jax.ShapeDtypeStruct((2, CS, SLAB), jnp.bfloat16)
    block = pl.BlockSpec((1, rows, SLAB), lambda p, r, role: (p, r, 0))
    return pl.pallas_call(
        slab_kernel,
        out_shape=(slab, slab),
        grid_spec=pltpu.PrefetchScalarGridSpec(
            num_scalar_prefetch=1,
            grid=(2, CS // rows),
            in_specs=[pl.BlockSpec((1, rows, 2 * HALF), lambda p, r, role: ((p + role[0]) % 2, r, 0))],
            out_specs=(block, block),
        ),
        cost_estimate=pl.CostEstimate(flops=0, bytes_accessed=5 << 20, transcendentals=0),
        name="slabs",
    )(role, field)


def tile_roll(block, by):
    return jnp.concatenate(
        [pltpu.roll(block[:, at : at + LANES], by, 1) for at in range(0, block.shape[1], LANES)], axis=1
    )


def pair_chunk(chunk, triple, weight, sigma, tau, z_odd):
    lane = lax.broadcasted_iota(jnp.int32, (CS, CHUNK), 1)
    low = lane % LANES < LANES // 2
    tiles = CHUNK // LANES
    before = lax.rem(chunk * tiles + SLAB // LANES - 1, SLAB // LANES)

    def load(ref):
        return jnp.concatenate(
            [
                ref[:, pl.ds(pl.multiple_of(before * LANES, LANES), LANES)],
                ref[:, pl.ds(pl.multiple_of(chunk * CHUNK, LANES), CHUNK + LANES)],
            ],
            axis=1,
        ).astype(jnp.float32)

    below, here, above = triple
    if z_odd:
        sources = [load(above) - load(below)]
    else:
        sources = [load(here), load(above) + load(below)]
    features = []
    for source in sources:
        features.append(source[:, LANES:-LANES].astype(jnp.bfloat16))
        summed = source[:, LANES:] + sigma * source[:, :-LANES]
        chosen = jnp.where(low, summed[:, LANES:], summed[:, :-LANES])
        features.append(tile_roll(chosen, LANES // 2).astype(jnp.bfloat16))
    stacked = jnp.concatenate(features, axis=0)
    total = jnp.dot(weight, stacked, preferred_element_type=jnp.float32)
    centre, side = total[:CS], total[CS:]
    swapped = tile_roll(side, LANES // 2)
    right = tile_roll(jnp.where(lane % 64 == 0, swapped, side), LANES - 1)
    left = tile_roll(jnp.where(lane % 64 == 63, swapped, side), 1)
    return centre + right + tau * left


def conv_kernel(jobs, n_planes, n_accs, role_ref, *refs):
    role = role_ref[0]
    comp, odd = role // 2, role % 2
    gathered = comp ^ (1 + odd)
    reduced = comp ^ (2 - odd)
    pairs = [(comp, comp), (comp, reduced), (gathered, reduced), (gathered, comp)]
    weight_ref = refs[0]
    planes = refs[1 : 1 + n_planes]
    accs = refs[1 + n_planes : 1 + n_planes + n_accs]
    outs = refs[1 + n_planes + n_accs :]
    for triple, slot, acc, out in jobs:
        i, o = pairs[slot]

        def differ(at):
            return (i == at).astype(jnp.int32) != (o == at).astype(jnp.int32)

        tau = jnp.where(differ(1), -1.0, 1.0)
        sigma = jnp.where(differ(2), -1.0, 1.0)
        refs_here = tuple(planes[at] for at in triple)

        def run(z_odd, columns, slot=slot, acc=acc, out=out, refs_here=refs_here, tau=tau, sigma=sigma):
            def body(chunk, carry):
                weight = weight_ref[slot, :, :columns]
                value = pair_chunk(chunk, refs_here, weight, sigma, tau, z_odd)
                where = pl.ds(pl.multiple_of(chunk * CHUNK, CHUNK), CHUNK)
                if acc is not None:
                    value = value + accs[acc][:, where].astype(jnp.float32)
                outs[out][:, where] = value.astype(outs[out].dtype)
                return carry

            lax.fori_loop(0, HALF // CHUNK, body, 0)

        odd_in_z = differ(3)

        @pl.when(odd_in_z)
        def _():
            run(True, 2 * CS)

        @pl.when(jnp.logical_not(odd_in_z))
        def _():
            run(False, 4 * CS)


def conv(name, role, weight, planes, accs, jobs, out_types):
    vmem = pl.BlockSpec(memory_space=pltpu.VMEM)
    flops = len(jobs) * 2 * 256 * 512 * HALF
    size = sum(a.size * a.dtype.itemsize for a in (*planes, *accs)) + len(out_types) * CS * HALF * 4
    return pl.pallas_call(
        functools.partial(conv_kernel, jobs, len(planes), len(accs)),
        out_shape=tuple(jax.ShapeDtypeStruct((CS, HALF), t) for t in out_types),
        in_specs=[pl.BlockSpec(memory_space=pltpu.SMEM)] + [vmem] * (1 + len(planes) + len(accs)),
        out_specs=tuple(vmem for _ in out_types),
        compiler_params=pltpu.CompilerParams(vmem_limit_bytes=48 << 20),
        cost_estimate=pl.CostEstimate(flops=flops, bytes_accessed=size, transcendentals=0),
        name=name,
    )(role, weight, *planes, *accs)


def final_kernel(role_ref, *refs):
    own, others, out_ref = refs[:4], refs[4:8], refs[8]
    plane, side = pl.program_id(0), pl.program_id(1)
    for p in range(2):

        @pl.when((plane == p) & (side == 0))
        def _():
            out_ref[0] = (own[p][...].astype(jnp.float32) + own[2 + p][...].astype(jnp.float32)).astype(out_ref.dtype)

        @pl.when((plane == p) & (side == 1))
        def _():
            out_ref[0] = (others[p][...].astype(jnp.float32) + others[2 + p][...].astype(jnp.float32)).astype(
                out_ref.dtype
            )


def final(role, own, others):
    def at(plane, side, role):
        odd = role[0] % 2
        return ((plane + odd) % 2, 0, (side + odd) % 2)

    vmem = pl.BlockSpec(memory_space=pltpu.VMEM)
    return pl.pallas_call(
        final_kernel,
        out_shape=jax.ShapeDtypeStruct((2, CS, 2 * HALF), jnp.bfloat16),
        grid_spec=pltpu.PrefetchScalarGridSpec(
            num_scalar_prefetch=1,
            grid=(2, 2),
            in_specs=[vmem] * 8,
            out_specs=pl.BlockSpec((1, CS, HALF), at),
        ),
        compiler_params=pltpu.CompilerParams(vmem_limit_bytes=48 << 20),
        cost_estimate=pl.CostEstimate(flops=0, bytes_accessed=8 << 20, transcendentals=0),
        name="final",
    )(role, *own, *others)


def shards(tensor_field, radial):
    n_space, n_chan = lax.axis_size("space"), lax.axis_size("chan")
    sub = n_chan // 4
    chips = n_space // 2
    field = tensor_field
    if sub > 1:
        groups = [[g * sub + h for h in range(sub)] for g in range(4)]
        field = lax.all_gather(field, "chan", axis_index_groups=groups, axis=1, tiled=True)

    def permute(value, place):
        pairs = []
        for s in range(n_space):
            for c in range(4):
                to_s, to_c = place(s // 2, s % 2, c)
                for h in range(sub):
                    pairs.append((s * n_chan + c * sub + h, to_s * n_chan + to_c * sub + h))
        return lax.ppermute(value, ("space", "chan"), pairs)

    def outward(z, k):
        return (z + (1 if k else -1)) % chips

    def gather_group(k, c):
        return c ^ (2 if k else 1)

    def reduce_group(k, c):
        return c ^ (1 if k else 2)

    role = ((lax.axis_index("chan") // sub) * 2 + lax.axis_index("space") % 2).astype(jnp.int32).reshape(1)

    keep, give = slabs(role, field)
    gather_near = permute(keep, lambda z, k, c: (2 * z + k, gather_group(k, c)))
    halo_near = permute(give[0], lambda z, k, c: (2 * outward(z, k) + 1 - k, c))
    halo_far = permute(keep[0], lambda z, k, c: (2 * outward(z, k) + k, c))
    gather_far = permute(give, lambda z, k, c: (2 * z + 1 - k, gather_group(1 - k, c)))
    other = permute(give, lambda z, k, c: (2 * z + 1 - k, c))
    weight = weights(role, radial)

    own = [halo_near, keep[0], keep[1], other[1], other[0], halo_far]
    f32, bf16 = jnp.float32, jnp.bfloat16
    kept, lent = {}, {}
    kept[2], kept[3], lent[2], lent[3] = conv(
        "own_inner", role, weight, own[1:5], [],
        [((0, 1, 2), 0, None, 0), ((1, 2, 3), 0, None, 1), ((0, 1, 2), 1, None, 2), ((1, 2, 3), 1, None, 3)],
        [f32] * 4,
    )
    halos = permute(jnp.stack([halo_near, halo_far]), lambda z, k, c: (2 * z + k, gather_group(k, c)))
    near = [halos[0], gather_near[0], gather_near[1], gather_far[1], gather_far[0], halos[1]]

    def reduce_near(value):
        return permute(value, lambda z, k, c: (2 * z + k, reduce_group(k, c)))

    def reduce_far(value):
        return permute(value, lambda z, k, c: (2 * z + 1 - k, reduce_group(k, c)))

    def swap(value):
        return permute(value, lambda z, k, c: (2 * z + 1 - k, c))

    sent2, sent3 = conv(
        "sent_inner", role, weight, near[1:5], [lent[2], lent[3]],
        [((0, 1, 2), 2, 0, 0), ((1, 2, 3), 2, 1, 1)], [bf16] * 2,
    )
    got_inner_near = reduce_near(sent2)
    got_inner_far = reduce_far(sent3)
    kept[1], kept[4], lent[1], lent[4] = conv(
        "own_boundary", role, weight, own, [],
        [((0, 1, 2), 0, None, 0), ((3, 4, 5), 0, None, 1), ((0, 1, 2), 1, None, 2), ((3, 4, 5), 1, None, 3)],
        [f32] * 4,
    )
    sent1, sent4 = conv(
        "sent_boundary", role, weight, near, [lent[1], lent[4]],
        [((0, 1, 2), 2, 0, 0), ((3, 4, 5), 2, 1, 1)], [bf16] * 2,
    )
    got_boundary_near = reduce_near(sent1)
    got_boundary_far = reduce_far(sent4)
    total2, total3, total1, total4 = conv(
        "kept", role, weight, near, [kept[2], kept[3], kept[1], kept[4]],
        [((1, 2, 3), 3, 0, 0), ((2, 3, 4), 3, 1, 1), ((0, 1, 2), 3, 2, 2), ((3, 4, 5), 3, 3, 3)],
        [f32, bf16, f32, bf16],
    )
    crossed = swap(jnp.stack([total4, total3]))
    out = final(
        role,
        [total1, total2, got_boundary_near, got_inner_near],
        [crossed[0], crossed[1], got_boundary_far, got_inner_far],
    )
    if sub > 1:
        out = lax.dynamic_slice_in_dim(out, lax.axis_index("chan") % sub * tensor_field.shape[1], tensor_field.shape[1], 1)
    return out


def solution(mesh):
    placed = (P("space", "chan", None), P())
    return jax.shard_map(
        shards, mesh=mesh, in_specs=placed, out_specs=P("space", "chan", None), check_vma=False
    )
```

```python
import functools

import jax
import jax.numpy as jnp
import numpy as np
from jax import lax
from jax.experimental import pallas as pl
from jax.experimental.pallas import tpu as pltpu
from jax.sharding import PartitionSpec as P


CS = 128
LANES = 128
HALF = 2048
ROW = 64
SLAB = HALF + 2 * ROW
CHUNK = 512


def weight_tables():
    index = np.zeros((8, 4, 8, 2), np.int32)
    scale = np.zeros((8, 4, 8, 2), np.float32)
    for comp in range(4):
        for odd in range(2):
            gathered = comp ^ (2 if odd else 1)
            reduced = comp ^ (1 if odd else 2)
            pairs = [(comp, comp), (comp, reduced), (gathered, reduced), (gathered, comp)]
            for slot, (i, o) in enumerate(pairs):
                z_odd = (i == 3) != (o == 3)
                for t in range(2):
                    for f in range(4):
                        if z_odd and f >= 2:
                            continue
                        d = (t, f % 2, 1 if (z_odd or f >= 2) else 0)
                        s = sum(d)
                        u = np.float32(np.array(d) / np.sqrt(max(s, 1)))
                        sign = np.float32(-1.0 if (z_odd and odd) else 1.0)
                        kind, first, second = 0, np.float32(0.0), np.float32(0.0)
                        if i == 0 and o == 0:
                            kind, first = 0, np.float32(1.0)
                        elif i == 0:
                            kind, first = 2, u[o - 1]
                        elif o == 0:
                            kind, first = 3, u[i - 1]
                        else:
                            kind = 1
                            first = np.float32(1.0 if i == o else 0.0)
                            second = u[i - 1] * u[o - 1]
                        index[comp * 2 + odd, slot, t * 4 + f] = (kind * 4 + s, 16 + s)
                        scale[comp * 2 + odd, slot, t * 4 + f] = (sign * first, sign * second)
    return index.reshape(8, 64), scale.reshape(8, 64)


def weights_kernel(role_ref, index_ref, scale_ref, radial_ref, out_ref):
    role = role_ref[0]
    for slot in range(4):
        for t in range(2):
            for f in range(4):
                at = (slot * 8 + t * 4 + f) * 2
                first = radial_ref[index_ref[role, at]].astype(jnp.float32) * scale_ref[role, at]
                second = radial_ref[index_ref[role, at + 1]].astype(jnp.float32) * scale_ref[role, at + 1]
                out_ref[slot, f * CS : (f + 1) * CS, t * CS : (t + 1) * CS] = (first + second).astype(jnp.bfloat16)


def weights(role, radial):
    index, scale = weight_tables()
    smem = pl.BlockSpec(memory_space=pltpu.SMEM)
    vmem = pl.BlockSpec(memory_space=pltpu.VMEM)
    return pl.pallas_call(
        weights_kernel,
        out_shape=jax.ShapeDtypeStruct((4, 4 * CS, 2 * CS), jnp.bfloat16),
        in_specs=[smem, smem, smem, vmem],
        out_specs=vmem,
        cost_estimate=pl.CostEstimate(flops=0, bytes_accessed=4 << 20, transcendentals=0),
        name="weights",
    )(role, jnp.asarray(index), jnp.asarray(scale), radial.reshape(20, CS, CS))


def turn_kernel(role_ref, field_ref, keep_ref, give_ref, keep_edge_ref, give_edge_ref):
    odd, plane = role_ref[0] % 2, pl.program_id(0)
    turned = jnp.transpose(field_ref[0])
    halves = [
        [turned[2 * HALF - ROW :], turned[:HALF], turned[HALF : HALF + ROW]],
        [turned[HALF - ROW : HALF], turned[HALF:], turned[:ROW]],
    ]
    for parity in range(2):

        @pl.when(odd == parity)
        def _():
            for ref, edge, half in ((keep_ref, keep_edge_ref, parity), (give_ref, give_edge_ref, 1 - parity)):
                for value, at in zip(halves[half], (0, ROW, ROW + HALF)):
                    ref[0, at : at + value.shape[0]] = value

                @pl.when(plane == 0)
                def _():
                    for value, at in zip(halves[half], (0, ROW, ROW + HALF)):
                        edge[at : at + value.shape[0]] = value


def turn(role, field):
    slab = jax.ShapeDtypeStruct((2, SLAB, CS), jnp.bfloat16)
    edge = jax.ShapeDtypeStruct((SLAB, CS), jnp.bfloat16)
    block = pl.BlockSpec((1, SLAB, CS), lambda p, role: (p, 0, 0))
    edge_block = pl.BlockSpec((SLAB, CS), lambda p, role: (0, 0))
    return pl.pallas_call(
        turn_kernel,
        out_shape=(slab, slab, edge, edge),
        grid_spec=pltpu.PrefetchScalarGridSpec(
            num_scalar_prefetch=1,
            grid=(2,),
            in_specs=[pl.BlockSpec((1, CS, 2 * HALF), lambda p, role: ((p + role[0]) % 2, 0, 0))],
            out_specs=(block, block, edge_block, edge_block),
        ),
        compiler_params=pltpu.CompilerParams(vmem_limit_bytes=32 << 20),
        cost_estimate=pl.CostEstimate(flops=0, bytes_accessed=6 << 20, transcendentals=0),
        name="turn",
    )(role, field)


def pair_chunk(start, triple, weight, sigma, tau, z_odd):
    def load(ref):
        return ref[start : start + CHUNK + 2 * ROW, :].astype(jnp.float32)

    below, here, above = triple
    if z_odd:
        sources = [load(above) - load(below)]
    else:
        sources = [load(here), load(above) + load(below)]
    features = []
    for source in sources:
        features.append(source[ROW : ROW + CHUNK].astype(jnp.bfloat16))
        features.append((source[2 * ROW :] + sigma * source[:CHUNK]).astype(jnp.bfloat16))
    total = jnp.dot(jnp.concatenate(features, axis=1), weight, preferred_element_type=jnp.float32)
    centre, side = total[:, :CS], total[:, CS:].reshape(CHUNK // ROW, ROW, CS)
    right = pltpu.roll(side, ROW - 1, 1).reshape(CHUNK, CS)
    left = pltpu.roll(side, 1, 1).reshape(CHUNK, CS)
    return centre + right + tau * left


def conv_kernel(jobs, stacks, n_accs, role_ref, weight_ref, *refs):
    role = role_ref[0]
    comp, odd = role // 2, role % 2
    gathered = comp ^ (1 + odd)
    reduced = comp ^ (2 - odd)
    pairs = [(comp, comp), (comp, reduced), (gathered, reduced), (gathered, comp)]
    planes = []
    for ref, stack in zip(refs, stacks):
        planes.append([ref] if stack == 0 else [ref.at[at] for at in range(stack)])
    accs = refs[len(stacks) : len(stacks) + n_accs]
    outs = refs[len(refs) - len(jobs) :]
    for (triple, slot, acc), out in zip(jobs, outs):
        i, o = pairs[slot]

        def differ(at):
            return (i == at).astype(jnp.int32) != (o == at).astype(jnp.int32)

        tau = jnp.where(differ(1), -1.0, 1.0)
        sigma = jnp.where(differ(2), -1.0, 1.0)
        three = [planes[at][index] for at, index in triple]

        def run(z_odd, rows):
            for start in range(0, HALF, CHUNK):
                value = pair_chunk(start, three, weight_ref[slot, :rows, :], sigma, tau, z_odd)
                if acc is not None:
                    value = value + accs[acc][start : start + CHUNK].astype(jnp.float32)
                out[start : start + CHUNK] = value.astype(out.dtype)

        odd_in_z = differ(3)

        @pl.when(odd_in_z)
        def _():
            run(True, 2 * CS)

        @pl.when(jnp.logical_not(odd_in_z))
        def _():
            run(False, 4 * CS)


def conv(name, role, weight, planes, accs, jobs, types, after=()):
    vmem = pl.BlockSpec(memory_space=pltpu.VMEM)
    flops = len(jobs) * 2 * 256 * 512 * HALF
    size = sum(a.size * a.dtype.itemsize for a in (*planes, *accs)) + len(jobs) * CS * HALF * 4
    stacks = [a.shape[0] if a.ndim == 3 else 0 for a in planes]
    return pl.pallas_call(
        functools.partial(conv_kernel, jobs, stacks, len(accs)),
        out_shape=tuple(jax.ShapeDtypeStruct((HALF, CS), t) for t in types),
        in_specs=[pl.BlockSpec(memory_space=pltpu.SMEM)]
        + [vmem] * (1 + len(planes) + len(accs))
        + [pl.BlockSpec(memory_space=pl.ANY)] * len(after),
        out_specs=tuple(vmem for _ in types),
        compiler_params=pltpu.CompilerParams(vmem_limit_bytes=40 << 20),
        cost_estimate=pl.CostEstimate(flops=flops, bytes_accessed=size, transcendentals=0),
        name=name,
    )(role, weight, *planes, *accs, *after)


def final_kernel(role_ref, *refs):
    own, others, out_ref = refs[:4], refs[4:7], refs[7]
    plane, side = pl.program_id(0), pl.program_id(1)

    def put(first, second):
        total = first.astype(jnp.float32) + second.astype(jnp.float32)
        out_ref[0] = jnp.transpose(total.astype(out_ref.dtype))

    for p in range(2):

        @pl.when((plane == p) & (side == 0))
        def _():
            put(own[p][...], own[2 + p][...])

        @pl.when((plane == p) & (side == 1))
        def _():
            put(others[0][p], others[1 + p][...])


def final(role, own, others):
    def at(plane, side, role):
        odd = role[0] % 2
        return ((plane + odd) % 2, 0, (side + odd) % 2)

    vmem = pl.BlockSpec(memory_space=pltpu.VMEM)
    return pl.pallas_call(
        final_kernel,
        out_shape=jax.ShapeDtypeStruct((2, CS, 2 * HALF), jnp.bfloat16),
        grid_spec=pltpu.PrefetchScalarGridSpec(
            num_scalar_prefetch=1,
            grid=(2, 2),
            in_specs=[vmem] * 7,
            out_specs=pl.BlockSpec((1, CS, HALF), at),
        ),
        compiler_params=pltpu.CompilerParams(vmem_limit_bytes=40 << 20),
        cost_estimate=pl.CostEstimate(flops=0, bytes_accessed=8 << 20, transcendentals=0),
        name="final",
    )(role, *own, *others)


def shards(tensor_field, radial):
    n_space, n_chan = lax.axis_size("space"), lax.axis_size("chan")
    sub = n_chan // 4
    chips = n_space // 2
    field = tensor_field
    if sub > 1:
        groups = [[g * sub + h for h in range(sub)] for g in range(4)]
        field = lax.all_gather(field, "chan", axis_index_groups=groups, axis=1, tiled=True)

    def permute(value, place):
        pairs = []
        for s in range(n_space):
            for c in range(4):
                to_s, to_c = place(s // 2, s % 2, c)
                for h in range(sub):
                    pairs.append((s * n_chan + c * sub + h, to_s * n_chan + to_c * sub + h))
        return lax.ppermute(value, ("space", "chan"), pairs)

    def outward(z, k):
        return (z + (1 if k else -1)) % chips

    def gather_group(k, c):
        return c ^ (2 if k else 1)

    def reduce_group(k, c):
        return c ^ (1 if k else 2)

    role = ((lax.axis_index("chan") // sub) * 2 + lax.axis_index("space") % 2).astype(jnp.int32).reshape(1)

    def reduce_near(value):
        return permute(value, lambda z, k, c: (2 * z + k, reduce_group(k, c)))

    def reduce_far(value):
        return permute(value, lambda z, k, c: (2 * z + 1 - k, reduce_group(k, c)))

    def swap(value):
        return permute(value, lambda z, k, c: (2 * z + 1 - k, c))

    keep, give, keep_edge, give_edge = turn(role, field)
    gather_near = permute(keep, lambda z, k, c: (2 * z + k, gather_group(k, c)))
    halo_near = permute(give_edge, lambda z, k, c: (2 * outward(z, k) + 1 - k, c))
    halo_far = permute(keep_edge, lambda z, k, c: (2 * outward(z, k) + k, c))
    gather_far = permute(give, lambda z, k, c: (2 * z + 1 - k, gather_group(1 - k, c)))
    other = swap(give)
    weight = weights(role, radial)

    f32, bf16 = jnp.float32, jnp.bfloat16
    inner = {1: (0, 0), 2: (0, 1), 4: (1, 0), 3: (1, 1)}

    def around(plane, where):
        return tuple(where[at] for at in (plane - 1, plane, plane + 1))

    kept2, kept3, lent2, lent3 = conv(
        "own_inner", role, weight, [keep, other], [],
        [(around(2, inner), 0, None), (around(3, inner), 0, None), (around(2, inner), 1, None), (around(3, inner), 1, None)],
        [f32] * 4,
    )
    halo_near, halo_far, lent2, lent3 = lax.optimization_barrier((halo_near, halo_far, lent2, lent3))
    halos = permute(jnp.stack([halo_near, halo_far]), lambda z, k, c: (2 * z + k, gather_group(k, c)))
    sent2, sent3 = conv(
        "sent_inner", role, weight, [gather_near, gather_far], [lent2, lent3],
        [(around(2, inner), 2, 0), (around(3, inner), 2, 1)], [bf16] * 2,
    )
    got_inner_near = reduce_near(sent2)
    got_inner_far = reduce_far(sent3)
    own_all = inner | {0: (2, 0), 5: (3, 0)}
    kept1, kept4, lent1, lent4 = conv(
        "own_boundary", role, weight, [keep, other, halo_near, halo_far], [],
        [(around(1, own_all), 0, None), (around(4, own_all), 0, None), (around(1, own_all), 1, None), (around(4, own_all), 1, None)],
        [f32] * 4, after=[sent2],
    )
    near_all = inner | {0: (2, 0), 5: (2, 1)}
    sent1, sent4 = conv(
        "sent_boundary", role, weight, [gather_near, gather_far, halos], [lent1, lent4],
        [(around(1, near_all), 2, 0), (around(4, near_all), 2, 1)], [bf16] * 2,
    )
    got_boundary_near = reduce_near(sent1)
    got_boundary_far = reduce_far(sent4)
    total4, total3 = conv(
        "kept_far", role, weight, [gather_near, gather_far, halos], [kept4, kept3],
        [(around(4, near_all), 3, 0), (around(3, near_all), 3, 1)], [bf16] * 2, after=[sent1],
    )
    crossed = swap(jnp.stack([total4, total3]))
    total1, total2 = conv(
        "kept_near", role, weight, [gather_near, gather_far, halos], [kept1, kept2],
        [(around(1, near_all), 3, 0), (around(2, near_all), 3, 1)], [f32] * 2, after=[total4],
    )
    out = final(
        role,
        [total1, total2, got_boundary_near, got_inner_near],
        [crossed, got_boundary_far, got_inner_far],
    )
    if sub > 1:
        out = lax.dynamic_slice_in_dim(out, lax.axis_index("chan") % sub * tensor_field.shape[1], tensor_field.shape[1], 1)
    return out


def solution(mesh):
    placed = (P("space", "chan", None), P())
    return jax.shard_map(
        shards, mesh=mesh, in_specs=placed, out_specs=P("space", "chan", None), check_vma=False
    )
```

```python
import functools

import jax
import jax.numpy as jnp
import numpy as np
from jax import lax
from jax.experimental import pallas as pl
from jax.experimental.pallas import tpu as pltpu
from jax.sharding import PartitionSpec as P


CS = 128
LANES = 128
HALF = 2048
ROW = 64
SLAB = HALF + 2 * ROW
CHUNK = 512
TURN_VMEM = 60 << 20


def weight_tables():
    index = np.zeros((8, 4, 8, 2), np.int32)
    scale = np.zeros((8, 4, 8, 2), np.float32)
    for comp in range(4):
        for odd in range(2):
            gathered = comp ^ (2 if odd else 1)
            reduced = comp ^ (1 if odd else 2)
            pairs = [(comp, comp), (comp, reduced), (gathered, reduced), (gathered, comp)]
            for slot, (i, o) in enumerate(pairs):
                z_odd = (i == 3) != (o == 3)
                for t in range(2):
                    for f in range(4):
                        if z_odd and f >= 2:
                            continue
                        d = (t, f % 2, 1 if (z_odd or f >= 2) else 0)
                        s = sum(d)
                        u = np.float32(np.array(d) / np.sqrt(max(s, 1)))
                        sign = np.float32(-1.0 if (z_odd and odd) else 1.0)
                        kind, first, second = 0, np.float32(0.0), np.float32(0.0)
                        if i == 0 and o == 0:
                            kind, first = 0, np.float32(1.0)
                        elif i == 0:
                            kind, first = 2, u[o - 1]
                        elif o == 0:
                            kind, first = 3, u[i - 1]
                        else:
                            kind = 1
                            first = np.float32(1.0 if i == o else 0.0)
                            second = u[i - 1] * u[o - 1]
                        index[comp * 2 + odd, slot, t * 4 + f] = (kind * 4 + s, 16 + s)
                        scale[comp * 2 + odd, slot, t * 4 + f] = (sign * first, sign * second)
    return index.reshape(8, 64), scale.reshape(8, 64)


def weights_kernel(role_ref, index_ref, scale_ref, radial_ref, out_ref):
    role = role_ref[0]
    for slot in range(4):
        for t in range(2):
            for f in range(4):
                at = (slot * 8 + t * 4 + f) * 2
                first = radial_ref[index_ref[role, at]].astype(jnp.float32) * scale_ref[role, at]
                second = radial_ref[index_ref[role, at + 1]].astype(jnp.float32) * scale_ref[role, at + 1]
                out_ref[slot, f * CS : (f + 1) * CS, t * CS : (t + 1) * CS] = (first + second).astype(jnp.bfloat16)


def weights(role, radial):
    index, scale = weight_tables()
    smem = pl.BlockSpec(memory_space=pltpu.SMEM)
    vmem = pl.BlockSpec(memory_space=pltpu.VMEM)
    return pl.pallas_call(
        weights_kernel,
        out_shape=jax.ShapeDtypeStruct((4, 4 * CS, 2 * CS), jnp.bfloat16),
        in_specs=[smem, smem, smem, vmem],
        out_specs=vmem,
        cost_estimate=pl.CostEstimate(flops=0, bytes_accessed=4 << 20, transcendentals=0),
        name="weights",
    )(role, jnp.asarray(index), jnp.asarray(scale), radial.reshape(20, CS, CS))


def turn_kernel(role_ref, field_ref, keep_edge_ref, keep_inner_ref, give_ref, give_edge_ref):
    odd, plane = role_ref[0] % 2, pl.program_id(0)
    turned = jnp.transpose(field_ref[0])
    halves = [
        [turned[2 * HALF - ROW :], turned[:HALF], turned[HALF : HALF + ROW]],
        [turned[HALF - ROW : HALF], turned[HALF:], turned[:ROW]],
    ]

    def put(ref, half):
        for value, at in zip(halves[half], (0, ROW, ROW + HALF)):
            ref[at : at + value.shape[0]] = value

    for parity in range(2):

        @pl.when(odd == parity)
        def _():
            put(give_ref.at[0], 1 - parity)

            @pl.when(plane == 0)
            def _():
                put(keep_edge_ref, parity)
                put(give_edge_ref, 1 - parity)

            @pl.when(plane == 1)
            def _():
                put(keep_inner_ref, parity)


def turn(role, field):
    single = jax.ShapeDtypeStruct((SLAB, CS), jnp.bfloat16)
    single_block = pl.BlockSpec((SLAB, CS), lambda p, role: (0, 0))
    return pl.pallas_call(
        turn_kernel,
        out_shape=(single, single, jax.ShapeDtypeStruct((2, SLAB, CS), jnp.bfloat16), single),
        grid_spec=pltpu.PrefetchScalarGridSpec(
            num_scalar_prefetch=1,
            grid=(2,),
            in_specs=[pl.BlockSpec((1, CS, 2 * HALF), lambda p, role: ((p + role[0]) % 2, 0, 0))],
            out_specs=(single_block, single_block, pl.BlockSpec((1, SLAB, CS), lambda p, role: (p, 0, 0)), single_block),
        ),
        compiler_params=pltpu.CompilerParams(vmem_limit_bytes=TURN_VMEM),
        cost_estimate=pl.CostEstimate(flops=0, bytes_accessed=6 << 20, transcendentals=0),
        name="turn",
    )(role, field)


def pair_chunk(start, triple, weight, sigma, tau, z_odd):
    def load(ref):
        return ref[start : start + CHUNK + 2 * ROW, :].astype(jnp.float32)

    below, here, above = triple
    if z_odd:
        sources = [load(above) - load(below)]
    else:
        sources = [load(here), load(above) + load(below)]
    features = []
    for source in sources:
        features.append(source[ROW : ROW + CHUNK].astype(jnp.bfloat16))
        features.append((source[2 * ROW :] + sigma * source[:CHUNK]).astype(jnp.bfloat16))
    total = jnp.dot(jnp.concatenate(features, axis=1), weight, preferred_element_type=jnp.float32)
    centre, side = total[:, :CS], total[:, CS:].reshape(CHUNK // ROW, ROW, CS)
    right = pltpu.roll(side, ROW - 1, 1).reshape(CHUNK, CS)
    left = pltpu.roll(side, 1, 1).reshape(CHUNK, CS)
    return centre + right + tau * left


def conv_kernel(jobs, stacks, n_accs, role_ref, weight_ref, *refs):
    role = role_ref[0]
    comp, odd = role // 2, role % 2
    gathered = comp ^ (1 + odd)
    reduced = comp ^ (2 - odd)
    pairs = [(comp, comp), (comp, reduced), (gathered, reduced), (gathered, comp)]
    planes = []
    for ref, stack in zip(refs, stacks):
        planes.append([ref] if stack == 0 else [ref.at[at] for at in range(stack)])
    accs = refs[len(stacks) : len(stacks) + n_accs]
    outs = refs[len(refs) - len(jobs) :]
    for (triple, slot, acc), out in zip(jobs, outs):
        i, o = pairs[slot]

        def differ(at):
            return (i == at).astype(jnp.int32) != (o == at).astype(jnp.int32)

        tau = jnp.where(differ(1), -1.0, 1.0)
        sigma = jnp.where(differ(2), -1.0, 1.0)
        three = [planes[at][index] for at, index in triple]

        def run(z_odd, rows):
            for start in range(0, HALF, CHUNK):
                value = pair_chunk(start, three, weight_ref[slot, :rows, :], sigma, tau, z_odd)
                if acc is not None:
                    value = value + accs[acc][start : start + CHUNK].astype(jnp.float32)
                out[start : start + CHUNK] = value.astype(out.dtype)

        odd_in_z = differ(3)

        @pl.when(odd_in_z)
        def _():
            run(True, 2 * CS)

        @pl.when(jnp.logical_not(odd_in_z))
        def _():
            run(False, 4 * CS)


def conv(name, role, weight, planes, accs, jobs, types, after=()):
    vmem = pl.BlockSpec(memory_space=pltpu.VMEM)
    flops = len(jobs) * 2 * 256 * 512 * HALF
    size = sum(a.size * a.dtype.itemsize for a in (*planes, *accs)) + len(jobs) * CS * HALF * 4
    stacks = [a.shape[0] if a.ndim == 3 else 0 for a in planes]
    return pl.pallas_call(
        functools.partial(conv_kernel, jobs, stacks, len(accs)),
        out_shape=tuple(jax.ShapeDtypeStruct((HALF, CS), t) for t in types),
        in_specs=[pl.BlockSpec(memory_space=pltpu.SMEM)]
        + [vmem] * (1 + len(planes) + len(accs))
        + [pl.BlockSpec(memory_space=pl.ANY)] * len(after),
        out_specs=tuple(vmem for _ in types),
        compiler_params=pltpu.CompilerParams(vmem_limit_bytes=40 << 20),
        cost_estimate=pl.CostEstimate(flops=flops, bytes_accessed=size, transcendentals=0),
        name=name,
    )(role, weight, *planes, *accs, *after)


def final_kernel(role_ref, *refs):
    own, others, out_ref = refs[:4], refs[4:8], refs[8]
    plane, side = pl.program_id(0), pl.program_id(1)

    def put(first, second):
        total = first.astype(jnp.float32) + second.astype(jnp.float32)
        out_ref[0] = jnp.transpose(total.astype(out_ref.dtype))

    for p in range(2):

        @pl.when((plane == p) & (side == 0))
        def _():
            put(own[p][...], own[2 + p][...])

        @pl.when((plane == p) & (side == 1))
        def _():
            put(others[p][...], others[2 + p][...])


def final(role, own, others):
    def at(plane, side, role):
        odd = role[0] % 2
        return ((plane + odd) % 2, 0, (side + odd) % 2)

    vmem = pl.BlockSpec(memory_space=pltpu.VMEM)
    return pl.pallas_call(
        final_kernel,
        out_shape=jax.ShapeDtypeStruct((2, CS, 2 * HALF), jnp.bfloat16),
        grid_spec=pltpu.PrefetchScalarGridSpec(
            num_scalar_prefetch=1,
            grid=(2, 2),
            in_specs=[vmem] * 8,
            out_specs=pl.BlockSpec((1, CS, HALF), at),
        ),
        compiler_params=pltpu.CompilerParams(vmem_limit_bytes=40 << 20),
        cost_estimate=pl.CostEstimate(flops=0, bytes_accessed=8 << 20, transcendentals=0),
        name="final",
    )(role, *own, *others)


def shards(tensor_field, radial):
    n_space, n_chan = lax.axis_size("space"), lax.axis_size("chan")
    sub = n_chan // 4
    chips = n_space // 2
    field = tensor_field
    if sub > 1:
        groups = [[g * sub + h for h in range(sub)] for g in range(4)]
        field = lax.all_gather(field, "chan", axis_index_groups=groups, axis=1, tiled=True)

    def permute(value, place):
        pairs = []
        for s in range(n_space):
            for c in range(4):
                to_s, to_c = place(s // 2, s % 2, c)
                for h in range(sub):
                    pairs.append((s * n_chan + c * sub + h, to_s * n_chan + to_c * sub + h))
        return lax.ppermute(value, ("space", "chan"), pairs)

    def outward(z, k):
        return (z + (1 if k else -1)) % chips

    def gather_group(k, c):
        return c ^ (2 if k else 1)

    def reduce_group(k, c):
        return c ^ (1 if k else 2)

    role = ((lax.axis_index("chan") // sub) * 2 + lax.axis_index("space") % 2).astype(jnp.int32).reshape(1)

    def reduce_near(value):
        return permute(value, lambda z, k, c: (2 * z + k, reduce_group(k, c)))

    def reduce_far(value):
        return permute(value, lambda z, k, c: (2 * z + 1 - k, reduce_group(k, c)))

    def swap(value):
        return permute(value, lambda z, k, c: (2 * z + 1 - k, c))

    def gather_near(value):
        return permute(value, lambda z, k, c: (2 * z + k, gather_group(k, c)))

    def from_far(value):
        return permute(value, lambda z, k, c: (2 * outward(z, k) + k, c))

    f32, bf16 = jnp.float32, jnp.bfloat16
    keep_edge, keep_inner, give, give_edge = turn(role, field)
    near_edge = gather_near(keep_edge)
    halo_near = permute(give_edge, lambda z, k, c: (2 * outward(z, k) + 1 - k, c))
    halo_far = from_far(keep_edge)
    near_inner = gather_near(keep_inner)
    near_others = permute(give, lambda z, k, c: (2 * z + 1 - k, gather_group(1 - k, c)))
    others = swap(give)
    weight = weights(role, radial)

    inner = {1: (0, 0), 2: (1, 0), 4: (2, 0), 3: (2, 1)}
    all_planes = inner | {0: (3, 0), 5: (4, 0)}

    def jobs(of, *wanted):
        return [(tuple(of[at] for at in (plane - 1, plane, plane + 1)), slot, acc) for plane, slot, acc in wanted]

    own = [keep_edge, keep_inner, others]
    kept2, kept3, lent2, lent3 = conv(
        "own_inner", role, weight, own, [],
        jobs(inner, (2, 0, None), (3, 0, None), (2, 1, None), (3, 1, None)), [f32] * 4,
    )
    far_halo = from_far(near_edge)
    near_halo = gather_near(halo_near)
    near = [near_edge, near_inner, near_others]
    sent2, sent3 = conv(
        "sent_inner", role, weight, near, [lent2, lent3], jobs(inner, (2, 2, 0), (3, 2, 1)), [bf16] * 2,
    )
    got2, got3 = reduce_near(sent2), reduce_far(sent3)
    kept1, kept4, lent1, lent4 = conv(
        "own_boundary", role, weight, [*own, halo_near, halo_far], [],
        jobs(all_planes, (1, 0, None), (4, 0, None), (1, 1, None), (4, 1, None)), [f32] * 4, after=[sent2],
    )
    total2, total3 = conv(
        "kept_inner", role, weight, near, [kept2, kept3], jobs(inner, (2, 3, 0), (3, 3, 1)), [f32, bf16], after=[sent2],
    )
    crossed3 = swap(total3)
    near = [*near, near_halo, far_halo]
    sent1, sent4, total4 = conv(
        "sent_boundary", role, weight, near, [lent1, lent4, kept4],
        jobs(all_planes, (1, 2, 0), (4, 2, 1), (4, 3, 2)), [bf16] * 3, after=[total2],
    )
    got1, got4 = reduce_near(sent1), reduce_far(sent4)
    crossed4 = swap(total4)
    total1, = conv(
        "kept_boundary", role, weight, near, [kept1], jobs(all_planes, (1, 3, 0)), [f32], after=[sent1, got2, got3],
    )
    out = final(role, [total1, total2, got1, got2], [crossed4, crossed3, got4, got3])
    if sub > 1:
        out = lax.dynamic_slice_in_dim(out, lax.axis_index("chan") % sub * tensor_field.shape[1], tensor_field.shape[1], 1)
    return out


def solution(mesh):
    placed = (P("space", "chan", None), P())
    return jax.shard_map(
        shards, mesh=mesh, in_specs=placed, out_specs=P("space", "chan", None), check_vma=False
    )
```

```python
import functools

import jax
import jax.numpy as jnp
import numpy as np
from jax import lax
from jax.experimental import pallas as pl
from jax.experimental.pallas import tpu as pltpu
from jax.sharding import PartitionSpec as P


CS = 128
LANES = 128
HALF = 2048
ROW = 64
SLAB = HALF + 2 * ROW
CHUNK = 512
TURN_VMEM = 60 << 20
COST = pl.CostEstimate(flops=1000, bytes_accessed=1000, transcendentals=0)
LONG = pl.CostEstimate(flops=20 * 10**9, bytes_accessed=64 << 20, transcendentals=0)


def weight_tables():
    index = np.zeros((8, 4, 8, 2), np.int32)
    scale = np.zeros((8, 4, 8, 2), np.float32)
    for comp in range(4):
        for odd in range(2):
            gathered = comp ^ (2 if odd else 1)
            reduced = comp ^ (1 if odd else 2)
            pairs = [(comp, comp), (comp, reduced), (gathered, reduced), (gathered, comp)]
            for slot, (i, o) in enumerate(pairs):
                z_odd = (i == 3) != (o == 3)
                for t in range(2):
                    for f in range(4):
                        if z_odd and f >= 2:
                            continue
                        d = (t, f % 2, 1 if (z_odd or f >= 2) else 0)
                        s = sum(d)
                        u = np.float32(np.array(d) / np.sqrt(max(s, 1)))
                        sign = np.float32(-1.0 if (z_odd and odd) else 1.0)
                        kind, first, second = 0, np.float32(0.0), np.float32(0.0)
                        if i == 0 and o == 0:
                            kind, first = 0, np.float32(1.0)
                        elif i == 0:
                            kind, first = 2, u[o - 1]
                        elif o == 0:
                            kind, first = 3, u[i - 1]
                        else:
                            kind = 1
                            first = np.float32(1.0 if i == o else 0.0)
                            second = u[i - 1] * u[o - 1]
                        index[comp * 2 + odd, slot, t * 4 + f] = (kind * 4 + s, 16 + s)
                        scale[comp * 2 + odd, slot, t * 4 + f] = (sign * first, sign * second)
    return index.reshape(8, 64), scale.reshape(8, 64)


def weights_kernel(role_ref, index_ref, scale_ref, radial_ref, out_ref):
    role = role_ref[0]
    for slot in range(4):
        for t in range(2):
            for f in range(4):
                at = (slot * 8 + t * 4 + f) * 2
                first = radial_ref[index_ref[role, at]].astype(jnp.float32) * scale_ref[role, at]
                second = radial_ref[index_ref[role, at + 1]].astype(jnp.float32) * scale_ref[role, at + 1]
                out_ref[slot, f * CS : (f + 1) * CS, t * CS : (t + 1) * CS] = (first + second).astype(jnp.bfloat16)


def weights(role, radial):
    index, scale = weight_tables()
    smem = pl.BlockSpec(memory_space=pltpu.SMEM)
    vmem = pl.BlockSpec(memory_space=pltpu.VMEM)
    return pl.pallas_call(
        weights_kernel,
        out_shape=jax.ShapeDtypeStruct((4, 4 * CS, 2 * CS), jnp.bfloat16),
        in_specs=[smem, smem, smem, vmem],
        out_specs=vmem,
        cost_estimate=COST,
        name="weights",
    )(role, jnp.asarray(index), jnp.asarray(scale), radial.reshape(20, CS, CS))


def turn_kernel(role_ref, field_ref, keep_ref, give_ref, keep_edge_ref, give_edge_ref, raw, turned, in_sems, out_sems):
    odd = role_ref[0] % 2
    quarter = HALF // 2
    loads, stores = [], []
    for p in range(2):
        for q in range(4):
            cells = slice(q * quarter, (q + 1) * quarter)
            copy = pltpu.make_async_copy(
                field_ref.at[(p + odd) % 2, :, cells], raw.at[p, :, cells], in_sems.at[p * 4 + q]
            )
            copy.start()
            loads.append(copy)
    for p in range(2):
        for q in range(4):
            loads[p * 4 + q].wait()
            block = jnp.transpose(raw[p, :, q * quarter : (q + 1) * quarter])
            turned[p, ROW + q * quarter : ROW + (q + 1) * quarter] = block
            if q == 0:
                turned[p, ROW + 2 * HALF :] = block[:ROW]
            if q == 3:
                turned[p, :ROW] = block[-ROW:]
        kept = turned.at[p, pl.ds(pl.multiple_of(odd * HALF, HALF), SLAB)]
        given = turned.at[p, pl.ds(pl.multiple_of((1 - odd) * HALF, HALF), SLAB)]
        wanted = [(given, give_ref.at[p]), (kept, keep_ref.at[p])]
        if p == 0:
            wanted += [(given, give_edge_ref), (kept, keep_edge_ref)]
        for source, target in wanted:
            copy = pltpu.make_async_copy(source, target, out_sems.at[len(stores)])
            copy.start()
            stores.append(copy)
    for copy in stores:
        copy.wait()


def turn(role, field):
    single = jax.ShapeDtypeStruct((SLAB, CS), jnp.bfloat16)
    double = jax.ShapeDtypeStruct((2, SLAB, CS), jnp.bfloat16)
    hbm = pl.BlockSpec(memory_space=pl.ANY)
    return pl.pallas_call(
        turn_kernel,
        out_shape=(double, double, single, single),
        in_specs=[pl.BlockSpec(memory_space=pltpu.SMEM), hbm],
        out_specs=(hbm,) * 4,
        scratch_shapes=[
            pltpu.VMEM((2, CS, 2 * HALF), jnp.bfloat16),
            pltpu.VMEM((2, 2 * HALF + 2 * ROW, CS), jnp.bfloat16),
            pltpu.SemaphoreType.DMA((8,)),
            pltpu.SemaphoreType.DMA((6,)),
        ],
        compiler_params=pltpu.CompilerParams(vmem_limit_bytes=TURN_VMEM),
        cost_estimate=COST,
        name="turn",
    )(role, field)


def pair_chunk(start, triple, weight, sigma, tau, z_odd):
    def load(ref):
        return ref[start : start + CHUNK + 2 * ROW, :].astype(jnp.float32)

    below, here, above = triple
    if z_odd:
        sources = [load(above) - load(below)]
    else:
        sources = [load(here), load(above) + load(below)]
    features = []
    for source in sources:
        features.append(source[ROW : ROW + CHUNK].astype(jnp.bfloat16))
        features.append((source[2 * ROW :] + sigma * source[:CHUNK]).astype(jnp.bfloat16))
    total = jnp.dot(jnp.concatenate(features, axis=1), weight, preferred_element_type=jnp.float32)
    centre, side = total[:, :CS], total[:, CS:].reshape(CHUNK // ROW, ROW, CS)
    right = pltpu.roll(side, ROW - 1, 1).reshape(CHUNK, CS)
    left = pltpu.roll(side, 1, 1).reshape(CHUNK, CS)
    return centre + right + tau * left


def conv_kernel(jobs, stacks, n_accs, n_outs, role_ref, weight_ref, *refs):
    role = role_ref[0]
    comp, odd = role // 2, role % 2
    gathered = comp ^ (1 + odd)
    reduced = comp ^ (2 - odd)
    pairs = [(comp, comp), (comp, reduced), (gathered, reduced), (gathered, comp)]
    planes = []
    for ref, stack in zip(refs, stacks):
        planes.append([ref] if stack == 0 else [ref.at[at] for at in range(stack)])
    accs = refs[len(stacks) : len(stacks) + n_accs]
    outs = refs[len(refs) - n_outs :]
    if n_outs < len(jobs):
        outs = [*outs[:-1], outs[-1].at[0], outs[-1].at[1]]
    for (triple, slot, acc), out in zip(jobs, outs):
        i, o = pairs[slot]

        def differ(at):
            return (i == at).astype(jnp.int32) != (o == at).astype(jnp.int32)

        tau = jnp.where(differ(1), -1.0, 1.0)
        sigma = jnp.where(differ(2), -1.0, 1.0)
        three = [planes[at][index] for at, index in triple]

        def run(z_odd, rows):
            for start in range(0, HALF, CHUNK):
                value = pair_chunk(start, three, weight_ref[slot, :rows, :], sigma, tau, z_odd)
                if acc is not None:
                    value = value + accs[acc][start : start + CHUNK].astype(jnp.float32)
                out[start : start + CHUNK] = value.astype(out.dtype)

        odd_in_z = differ(3)

        @pl.when(odd_in_z)
        def _():
            run(True, 2 * CS)

        @pl.when(jnp.logical_not(odd_in_z))
        def _():
            run(False, 4 * CS)


def conv(name, role, weight, planes, accs, jobs, types, after=(), cost=COST):
    vmem = pl.BlockSpec(memory_space=pltpu.VMEM)
    stacks = [a.shape[0] if a.ndim == 3 else 0 for a in planes]
    return pl.pallas_call(
        functools.partial(conv_kernel, jobs, stacks, len(accs), len(types)),
        out_shape=tuple(
            jax.ShapeDtypeStruct((2, HALF, CS) if len(types) < len(jobs) and at == len(types) - 1 else (HALF, CS), t)
            for at, t in enumerate(types)
        ),
        in_specs=[pl.BlockSpec(memory_space=pltpu.SMEM)]
        + [vmem] * (1 + len(planes) + len(accs))
        + [pl.BlockSpec(memory_space=pl.ANY)] * len(after),
        out_specs=tuple(vmem for _ in types),
        compiler_params=pltpu.CompilerParams(vmem_limit_bytes=40 << 20),
        cost_estimate=cost,
        name=name,
    )(role, weight, *planes, *accs, *after)


def final_kernel(parts, role_ref, *refs):
    out_ref = refs[-1]
    for p in range(parts):

        @pl.when(pl.program_id(0) == p)
        def _():
            total = refs[p][...].astype(jnp.float32) + refs[parts + p][...].astype(jnp.float32)
            out_ref[0] = jnp.transpose(total.astype(out_ref.dtype))


def final(name, role, places, kept, got, out=None):
    def at(part, role):
        odd = role[0] % 2
        plane, side = (sum(jnp.where(part == p, place[d], 0) for p, place in enumerate(places)) for d in (0, 1))
        return ((plane + odd) % 2, 0, (side + odd) % 2)

    def whole(value):
        if isinstance(value, tuple):
            array, index = value
            return array, pl.BlockSpec((None, HALF, CS), lambda p, role, index=index: (index, 0, 0))
        return value, pl.BlockSpec((HALF, CS), lambda p, role: (0, 0))

    arrays, specs = zip(*[whole(value) for value in (*kept, *got)])
    if out is not None:
        arrays, specs = (*arrays, out), (*specs, pl.BlockSpec(memory_space=pl.ANY))
    return pl.pallas_call(
        functools.partial(final_kernel, len(places)),
        out_shape=jax.ShapeDtypeStruct((2, CS, 2 * HALF), jnp.bfloat16),
        grid_spec=pltpu.PrefetchScalarGridSpec(
            num_scalar_prefetch=1, grid=(len(places),), in_specs=list(specs), out_specs=pl.BlockSpec((1, CS, HALF), at)
        ),
        input_output_aliases={} if out is None else {len(arrays): 0},
        compiler_params=pltpu.CompilerParams(vmem_limit_bytes=40 << 20),
        cost_estimate=COST,
        name=name,
    )(role, *arrays)


def shards(tensor_field, radial):
    n_space, n_chan = lax.axis_size("space"), lax.axis_size("chan")
    sub = n_chan // 4
    chips = n_space // 2
    field = tensor_field
    if sub > 1:
        groups = [[g * sub + h for h in range(sub)] for g in range(4)]
        field = lax.all_gather(field, "chan", axis_index_groups=groups, axis=1, tiled=True)

    def permute(value, place):
        pairs = []
        for s in range(n_space):
            for c in range(4):
                to_s, to_c = place(s // 2, s % 2, c)
                for h in range(sub):
                    pairs.append((s * n_chan + c * sub + h, to_s * n_chan + to_c * sub + h))
        return lax.ppermute(value, ("space", "chan"), pairs)

    def outward(z, k):
        return (z + (1 if k else -1)) % chips

    def gather_group(k, c):
        return c ^ (2 if k else 1)

    def reduce_group(k, c):
        return c ^ (1 if k else 2)

    role = ((lax.axis_index("chan") // sub) * 2 + lax.axis_index("space") % 2).astype(jnp.int32).reshape(1)

    def reduce_near(value):
        return permute(value, lambda z, k, c: (2 * z + k, reduce_group(k, c)))

    def reduce_far(value):
        return permute(value, lambda z, k, c: (2 * z + 1 - k, reduce_group(k, c)))

    def swap(value):
        return permute(value, lambda z, k, c: (2 * z + 1 - k, c))

    def gather_near(value):
        return permute(value, lambda z, k, c: (2 * z + k, gather_group(k, c)))

    def from_far(value):
        return permute(value, lambda z, k, c: (2 * outward(z, k) + k, c))

    f32, bf16 = jnp.float32, jnp.bfloat16
    keep, give, keep_edge, give_edge = turn(role, field)
    near = gather_near(keep)
    halo_near = permute(give_edge, lambda z, k, c: (2 * outward(z, k) + 1 - k, c))
    halo_far = from_far(keep_edge)
    near_others = permute(give, lambda z, k, c: (2 * z + 1 - k, gather_group(1 - k, c)))
    others = swap(give)
    weight = weights(role, radial)

    inner = {1: (0, 0), 2: (0, 1), 4: (1, 0), 3: (1, 1)}
    all_planes = inner | {0: (2, 0), 5: (3, 0)}

    def jobs(of, *wanted):
        return [(tuple(of[at] for at in (plane - 1, plane, plane + 1)), slot, acc) for plane, slot, acc in wanted]

    own = [keep, others]
    kept2, kept3, lent2, lent3 = conv(
        "own_inner", role, weight, own, [],
        jobs(inner, (2, 0, None), (3, 0, None), (2, 1, None), (3, 1, None)), [f32] * 4,
    )
    kept2, near_ready, halo_ready = lax.optimization_barrier((kept2, near, halo_near))
    near_halo = gather_near(halo_ready)
    far_halo = from_far(near_ready[0])
    near = [near, near_others]
    sent2, sent3 = conv(
        "sent_inner", role, weight, near, [lent2, lent3], jobs(inner, (2, 2, 0), (3, 2, 1)), [bf16] * 2,
    )
    got2, got3 = reduce_near(sent2), reduce_far(sent3)
    kept1, kept4, lent1, lent4 = conv(
        "own_boundary", role, weight, [*own, halo_near, halo_far], [],
        jobs(all_planes, (1, 0, None), (4, 0, None), (1, 1, None), (4, 1, None)), [f32] * 4, after=[sent2],
    )
    near = [*near, near_halo, far_halo]
    sent1, = conv(
        "sent_near", role, weight, near[:3], [lent1], jobs(all_planes, (1, 2, 0)), [bf16],
    )
    sent4, total = conv(
        "far", role, weight, near, [lent4, kept4, kept3],
        jobs(all_planes, (4, 2, 0), (4, 3, 1), (3, 3, 2)), [bf16] * 2, after=[sent1],
    )
    got1, got4, crossed = reduce_near(sent1), reduce_far(sent4), swap(total)
    total1, total2 = conv(
        "kept_near", role, weight, near, [kept1, kept2],
        jobs(all_planes, (1, 3, 0), (2, 3, 1)), [f32] * 2, after=[sent1, got2, got3], cost=LONG,
    )
    out = final(
        "final", role, [(0, 0), (1, 0), (1, 1)], [total1, total2, (crossed, 1)], [got1, got2, got3]
    )
    out = final("final_edge", role, [(0, 1)], [(crossed, 0)], [got4], out)
    if sub > 1:
        out = lax.dynamic_slice_in_dim(out, lax.axis_index("chan") % sub * tensor_field.shape[1], tensor_field.shape[1], 1)
    return out


def solution(mesh):
    placed = (P("space", "chan", None), P())
    return jax.shard_map(
        shards, mesh=mesh, in_specs=placed, out_specs=P("space", "chan", None), check_vma=False
    )
```

```python
import functools

import jax
import jax.numpy as jnp
import numpy as np
from jax import lax
from jax.experimental import pallas as pl
from jax.experimental.pallas import tpu as pltpu
from jax.sharding import PartitionSpec as P


CS = 128
LANES = 128
HALF = 2048
ROW = 64
SLAB = HALF + 2 * ROW
CHUNK = 512
TURN_VMEM = 60 << 20
COST = pl.CostEstimate(flops=1000, bytes_accessed=1000, transcendentals=0)
LONG = pl.CostEstimate(flops=20 * 10**9, bytes_accessed=64 << 20, transcendentals=0)


def weight_tables():
    index = np.zeros((8, 4, 8, 2), np.int32)
    scale = np.zeros((8, 4, 8, 2), np.float32)
    for comp in range(4):
        for odd in range(2):
            gathered = comp ^ (2 if odd else 1)
            reduced = comp ^ (1 if odd else 2)
            pairs = [(comp, comp), (comp, reduced), (gathered, reduced), (gathered, comp)]
            for slot, (i, o) in enumerate(pairs):
                z_odd = (i == 3) != (o == 3)
                for t in range(2):
                    for f in range(4):
                        if z_odd and f >= 2:
                            continue
                        d = (t, f % 2, 1 if (z_odd or f >= 2) else 0)
                        s = sum(d)
                        u = np.float32(np.array(d) / np.sqrt(max(s, 1)))
                        sign = np.float32(-1.0 if (z_odd and odd) else 1.0)
                        kind, first, second = 0, np.float32(0.0), np.float32(0.0)
                        if i == 0 and o == 0:
                            kind, first = 0, np.float32(1.0)
                        elif i == 0:
                            kind, first = 2, u[o - 1]
                        elif o == 0:
                            kind, first = 3, u[i - 1]
                        else:
                            kind = 1
                            first = np.float32(1.0 if i == o else 0.0)
                            second = u[i - 1] * u[o - 1]
                        index[comp * 2 + odd, slot, t * 4 + f] = (kind * 4 + s, 16 + s)
                        scale[comp * 2 + odd, slot, t * 4 + f] = (sign * first, sign * second)
    return index.reshape(8, 64), scale.reshape(8, 64)


def weights_kernel(role_ref, index_ref, scale_ref, radial_ref, out_ref):
    role = role_ref[0]
    for slot in range(4):
        for t in range(2):
            for f in range(4):
                at = (slot * 8 + t * 4 + f) * 2
                first = radial_ref[index_ref[role, at]].astype(jnp.float32) * scale_ref[role, at]
                second = radial_ref[index_ref[role, at + 1]].astype(jnp.float32) * scale_ref[role, at + 1]
                out_ref[slot, f * CS : (f + 1) * CS, t * CS : (t + 1) * CS] = (first + second).astype(jnp.bfloat16)


def weights(role, radial):
    index, scale = weight_tables()
    smem = pl.BlockSpec(memory_space=pltpu.SMEM)
    vmem = pl.BlockSpec(memory_space=pltpu.VMEM)
    return pl.pallas_call(
        weights_kernel,
        out_shape=jax.ShapeDtypeStruct((4, 4 * CS, 2 * CS), jnp.bfloat16),
        in_specs=[smem, smem, smem, vmem],
        out_specs=vmem,
        cost_estimate=COST,
        name="weights",
    )(role, jnp.asarray(index), jnp.asarray(scale), radial.reshape(20, CS, CS))


def turn_kernel(
    role_ref, field_ref, keep_ref, give_ref, keep_edge_ref, give_edge_ref, give_inner_ref, raw, turned, in_sems, out_sems
):
    odd = role_ref[0] % 2
    quarter = HALF // 2
    loads, stores = [], []
    for p in range(2):
        for q in range(4):
            cells = slice(q * quarter, (q + 1) * quarter)
            copy = pltpu.make_async_copy(
                field_ref.at[(p + odd) % 2, :, cells], raw.at[p, :, cells], in_sems.at[p * 4 + q]
            )
            copy.start()
            loads.append(copy)
    for p in range(2):
        for q in range(4):
            loads[p * 4 + q].wait()
            block = jnp.transpose(raw[p, :, q * quarter : (q + 1) * quarter])
            turned[p, ROW + q * quarter : ROW + (q + 1) * quarter] = block
            if q == 0:
                turned[p, ROW + 2 * HALF :] = block[:ROW]
            if q == 3:
                turned[p, :ROW] = block[-ROW:]
        kept = turned.at[p, pl.ds(pl.multiple_of(odd * HALF, HALF), SLAB)]
        given = turned.at[p, pl.ds(pl.multiple_of((1 - odd) * HALF, HALF), SLAB)]
        wanted = [(given, give_ref.at[p]), (kept, keep_ref.at[p])]
        if p == 0:
            wanted += [(given, give_edge_ref), (kept, keep_edge_ref)]
        else:
            wanted += [(given, give_inner_ref)]
        for source, target in wanted:
            copy = pltpu.make_async_copy(source, target, out_sems.at[len(stores)])
            copy.start()
            stores.append(copy)
    for copy in stores:
        copy.wait()


def turn(role, field):
    single = jax.ShapeDtypeStruct((SLAB, CS), jnp.bfloat16)
    double = jax.ShapeDtypeStruct((2, SLAB, CS), jnp.bfloat16)
    hbm = pl.BlockSpec(memory_space=pl.ANY)
    return pl.pallas_call(
        turn_kernel,
        out_shape=(double, double, single, single, single),
        in_specs=[pl.BlockSpec(memory_space=pltpu.SMEM), hbm],
        out_specs=(hbm,) * 5,
        scratch_shapes=[
            pltpu.VMEM((2, CS, 2 * HALF), jnp.bfloat16),
            pltpu.VMEM((2, 2 * HALF + 2 * ROW, CS), jnp.bfloat16),
            pltpu.SemaphoreType.DMA((8,)),
            pltpu.SemaphoreType.DMA((7,)),
        ],
        compiler_params=pltpu.CompilerParams(vmem_limit_bytes=TURN_VMEM),
        cost_estimate=COST,
        name="turn",
    )(role, field)


def pair_chunk(start, triple, weight, sigma, tau, z_odd):
    def load(ref):
        return ref[start : start + CHUNK + 2 * ROW, :].astype(jnp.float32)

    below, here, above = triple
    if z_odd:
        sources = [load(above) - load(below)]
    else:
        sources = [load(here), load(above) + load(below)]
    features = []
    for source in sources:
        features.append(source[ROW : ROW + CHUNK].astype(jnp.bfloat16))
        features.append((source[2 * ROW :] + sigma * source[:CHUNK]).astype(jnp.bfloat16))
    total = jnp.dot(jnp.concatenate(features, axis=1), weight, preferred_element_type=jnp.float32)
    centre, side = total[:, :CS], total[:, CS:].reshape(CHUNK // ROW, ROW, CS)
    right = pltpu.roll(side, ROW - 1, 1).reshape(CHUNK, CS)
    left = pltpu.roll(side, 1, 1).reshape(CHUNK, CS)
    return centre + right + tau * left


def conv_kernel(jobs, stacks, n_accs, n_outs, role_ref, weight_ref, *refs):
    role = role_ref[0]
    comp, odd = role // 2, role % 2
    gathered = comp ^ (1 + odd)
    reduced = comp ^ (2 - odd)
    pairs = [(comp, comp), (comp, reduced), (gathered, reduced), (gathered, comp)]
    planes = []
    for ref, stack in zip(refs, stacks):
        planes.append([ref] if stack == 0 else [ref.at[at] for at in range(stack)])
    accs = refs[len(stacks) : len(stacks) + n_accs]
    outs = refs[len(refs) - n_outs :]
    if n_outs < len(jobs):
        outs = [*outs[:-1], outs[-1].at[0], outs[-1].at[1]]
    for (triple, slot, acc), out in zip(jobs, outs):
        i, o = pairs[slot]

        def differ(at):
            return (i == at).astype(jnp.int32) != (o == at).astype(jnp.int32)

        tau = jnp.where(differ(1), -1.0, 1.0)
        sigma = jnp.where(differ(2), -1.0, 1.0)
        three = [planes[at][index] for at, index in triple]

        def run(z_odd, rows):
            for start in range(0, HALF, CHUNK):
                value = pair_chunk(start, three, weight_ref[slot, :rows, :], sigma, tau, z_odd)
                if acc is not None:
                    value = value + accs[acc][start : start + CHUNK].astype(jnp.float32)
                out[start : start + CHUNK] = value.astype(out.dtype)

        odd_in_z = differ(3)

        @pl.when(odd_in_z)
        def _():
            run(True, 2 * CS)

        @pl.when(jnp.logical_not(odd_in_z))
        def _():
            run(False, 4 * CS)


def conv(name, role, weight, planes, accs, jobs, types, after=(), cost=COST):
    vmem = pl.BlockSpec(memory_space=pltpu.VMEM)
    stacks = [a.shape[0] if a.ndim == 3 else 0 for a in planes]
    return pl.pallas_call(
        functools.partial(conv_kernel, jobs, stacks, len(accs), len(types)),
        out_shape=tuple(
            jax.ShapeDtypeStruct((2, HALF, CS) if len(types) < len(jobs) and at == len(types) - 1 else (HALF, CS), t)
            for at, t in enumerate(types)
        ),
        in_specs=[pl.BlockSpec(memory_space=pltpu.SMEM)]
        + [vmem] * (1 + len(planes) + len(accs))
        + [pl.BlockSpec(memory_space=pl.ANY)] * len(after),
        out_specs=tuple(vmem for _ in types),
        compiler_params=pltpu.CompilerParams(vmem_limit_bytes=40 << 20),
        cost_estimate=cost,
        name=name,
    )(role, weight, *planes, *accs, *after)


def final_kernel(parts, role_ref, *refs):
    out_ref = refs[-1]
    for p in range(parts):

        @pl.when(pl.program_id(0) == p)
        def _():
            total = refs[p][...].astype(jnp.float32) + refs[parts + p][...].astype(jnp.float32)
            out_ref[0] = jnp.transpose(total.astype(out_ref.dtype))


def final(name, role, places, kept, got, out=None):
    def at(part, role):
        odd = role[0] % 2
        plane, side = (sum(jnp.where(part == p, place[d], 0) for p, place in enumerate(places)) for d in (0, 1))
        return ((plane + odd) % 2, 0, (side + odd) % 2)

    def whole(value):
        if isinstance(value, tuple):
            array, index = value
            return array, pl.BlockSpec((None, HALF, CS), lambda p, role, index=index: (index, 0, 0))
        return value, pl.BlockSpec((HALF, CS), lambda p, role: (0, 0))

    arrays, specs = zip(*[whole(value) for value in (*kept, *got)])
    if out is not None:
        arrays, specs = (*arrays, out), (*specs, pl.BlockSpec(memory_space=pl.ANY))
    return pl.pallas_call(
        functools.partial(final_kernel, len(places)),
        out_shape=jax.ShapeDtypeStruct((2, CS, 2 * HALF), jnp.bfloat16),
        grid_spec=pltpu.PrefetchScalarGridSpec(
            num_scalar_prefetch=1, grid=(len(places),), in_specs=list(specs), out_specs=pl.BlockSpec((1, CS, HALF), at)
        ),
        input_output_aliases={} if out is None else {len(arrays): 0},
        compiler_params=pltpu.CompilerParams(vmem_limit_bytes=40 << 20),
        cost_estimate=COST,
        name=name,
    )(role, *arrays)


def shards(tensor_field, radial):
    n_space, n_chan = lax.axis_size("space"), lax.axis_size("chan")
    sub = n_chan // 4
    chips = n_space // 2
    field = tensor_field
    if sub > 1:
        groups = [[g * sub + h for h in range(sub)] for g in range(4)]
        field = lax.all_gather(field, "chan", axis_index_groups=groups, axis=1, tiled=True)

    def permute(value, place):
        pairs = []
        for s in range(n_space):
            for c in range(4):
                to_s, to_c = place(s // 2, s % 2, c)
                for h in range(sub):
                    pairs.append((s * n_chan + c * sub + h, to_s * n_chan + to_c * sub + h))
        return lax.ppermute(value, ("space", "chan"), pairs)

    def outward(z, k):
        return (z + (1 if k else -1)) % chips

    def gather_group(k, c):
        return c ^ (2 if k else 1)

    def reduce_group(k, c):
        return c ^ (1 if k else 2)

    role = ((lax.axis_index("chan") // sub) * 2 + lax.axis_index("space") % 2).astype(jnp.int32).reshape(1)

    def reduce_near(value):
        return permute(value, lambda z, k, c: (2 * z + k, reduce_group(k, c)))

    def reduce_far(value):
        return permute(value, lambda z, k, c: (2 * z + 1 - k, reduce_group(k, c)))

    def swap(value):
        return permute(value, lambda z, k, c: (2 * z + 1 - k, c))

    def gather_near(value):
        return permute(value, lambda z, k, c: (2 * z + k, gather_group(k, c)))

    def from_far(value):
        return permute(value, lambda z, k, c: (2 * outward(z, k) + k, c))

    f32, bf16 = jnp.float32, jnp.bfloat16
    def gather_cross(value):
        return permute(value, lambda z, k, c: (2 * z + 1 - k, gather_group(1 - k, c)))

    keep, give, keep_edge, give_edge, give_inner = turn(role, field)
    near = gather_near(keep)
    halo_near = permute(give_edge, lambda z, k, c: (2 * outward(z, k) + 1 - k, c))
    halo_far = from_far(keep_edge)
    others = swap(give)
    weight, give_inner = lax.optimization_barrier((weights(role, radial), give_inner))
    near3 = gather_cross(give_inner)

    own_inner = {1: (0, 0), 2: (0, 1), 4: (1, 0), 3: (1, 1)}
    own_all = own_inner | {0: (2, 0), 5: (3, 0)}
    near_all = {1: (0, 0), 2: (0, 1), 3: (1, 0), 4: (2, 0), 0: (3, 0), 5: (4, 0)}

    def jobs(of, *wanted):
        return [(tuple(of[at] for at in (plane - 1, plane, plane + 1)), slot, acc) for plane, slot, acc in wanted]

    own = [keep, others]
    kept2, kept3, lent2, lent3 = conv(
        "own_inner", role, weight, own, [],
        jobs(own_inner, (2, 0, None), (3, 0, None), (2, 1, None), (3, 1, None)), [f32] * 4,
    )
    kept2, near, give_edge = lax.optimization_barrier((kept2, near, give_edge))
    near4 = gather_cross(give_edge)
    far_halo = from_far(near[0])
    sent2, = conv(
        "sent_2", role, weight, [near, near3], [lent2], jobs(near_all, (2, 2, 0)), [bf16], cost=LONG,
    )
    got2 = reduce_near(sent2)
    near_halo = gather_near(halo_near)
    near = [near, near3, near4]
    sent3, = conv(
        "sent_3", role, weight, near, [lent3], jobs(near_all, (3, 2, 0)), [bf16], after=[sent2],
    )
    got3 = reduce_far(sent3)
    kept1, kept4, lent1, lent4 = conv(
        "own_boundary", role, weight, [*own, halo_near, halo_far], [],
        jobs(own_all, (1, 0, None), (4, 0, None), (1, 1, None), (4, 1, None)), [f32] * 4, after=[sent3],
    )
    near = [*near, near_halo, far_halo]
    sent1, = conv(
        "sent_near", role, weight, near[:4], [lent1], jobs(near_all, (1, 2, 0)), [bf16],
    )
    sent4, total = conv(
        "far", role, weight, near, [lent4, kept4, kept3],
        jobs(near_all, (4, 2, 0), (4, 3, 1), (3, 3, 2)), [bf16] * 2, after=[sent1],
    )
    got1, got4, crossed = reduce_near(sent1), reduce_far(sent4), swap(total)
    total1, total2 = conv(
        "kept_near", role, weight, near, [kept1, kept2],
        jobs(near_all, (1, 3, 0), (2, 3, 1)), [f32] * 2, after=[sent1, got2, got3], cost=LONG,
    )
    out = final(
        "final", role, [(0, 0), (1, 0), (1, 1)], [total1, total2, (crossed, 1)], [got1, got2, got3]
    )
    out = final("final_edge", role, [(0, 1)], [(crossed, 0)], [got4], out)
    if sub > 1:
        out = lax.dynamic_slice_in_dim(out, lax.axis_index("chan") % sub * tensor_field.shape[1], tensor_field.shape[1], 1)
    return out


def solution(mesh):
    placed = (P("space", "chan", None), P())
    return jax.shard_map(
        shards, mesh=mesh, in_specs=placed, out_specs=P("space", "chan", None), check_vma=False
    )
```

```python
import functools

import jax
import jax.numpy as jnp
import numpy as np
from jax import lax
from jax.experimental import pallas as pl
from jax.experimental.pallas import tpu as pltpu
from jax.sharding import PartitionSpec as P


CS = 128
LANES = 128
HALF = 2048
ROW = 64
SLAB = HALF + 2 * ROW
CHUNK = 512
TURN_VMEM = 60 << 20
COST = pl.CostEstimate(flops=1000, bytes_accessed=1000, transcendentals=0)
LONG = pl.CostEstimate(flops=20 * 10**9, bytes_accessed=64 << 20, transcendentals=0)


def weight_tables():
    index = np.zeros((8, 4, 8, 2), np.int32)
    scale = np.zeros((8, 4, 8, 2), np.float32)
    for comp in range(4):
        for odd in range(2):
            gathered = comp ^ (2 if odd else 1)
            reduced = comp ^ (1 if odd else 2)
            pairs = [(comp, comp), (comp, reduced), (gathered, reduced), (gathered, comp)]
            for slot, (i, o) in enumerate(pairs):
                z_odd = (i == 3) != (o == 3)
                for t in range(2):
                    for f in range(4):
                        if z_odd and f >= 2:
                            continue
                        d = (t, f % 2, 1 if (z_odd or f >= 2) else 0)
                        s = sum(d)
                        u = np.float32(np.array(d) / np.sqrt(max(s, 1)))
                        sign = np.float32(-1.0 if (z_odd and odd) else 1.0)
                        kind, first, second = 0, np.float32(0.0), np.float32(0.0)
                        if i == 0 and o == 0:
                            kind, first = 0, np.float32(1.0)
                        elif i == 0:
                            kind, first = 2, u[o - 1]
                        elif o == 0:
                            kind, first = 3, u[i - 1]
                        else:
                            kind = 1
                            first = np.float32(1.0 if i == o else 0.0)
                            second = u[i - 1] * u[o - 1]
                        index[comp * 2 + odd, slot, t * 4 + f] = (kind * 4 + s, 16 + s)
                        scale[comp * 2 + odd, slot, t * 4 + f] = (sign * first, sign * second)
    return index.reshape(8, 64), scale.reshape(8, 64)


def weights_kernel(role_ref, index_ref, scale_ref, radial_ref, out_ref):
    role = role_ref[0]
    for slot in range(4):
        for t in range(2):
            for f in range(4):
                at = (slot * 8 + t * 4 + f) * 2
                first = radial_ref[index_ref[role, at]].astype(jnp.float32) * scale_ref[role, at]
                second = radial_ref[index_ref[role, at + 1]].astype(jnp.float32) * scale_ref[role, at + 1]
                out_ref[slot, f * CS : (f + 1) * CS, t * CS : (t + 1) * CS] = (first + second).astype(jnp.bfloat16)


def weights(role, radial):
    index, scale = weight_tables()
    smem = pl.BlockSpec(memory_space=pltpu.SMEM)
    vmem = pl.BlockSpec(memory_space=pltpu.VMEM)
    return pl.pallas_call(
        weights_kernel,
        out_shape=jax.ShapeDtypeStruct((4, 4 * CS, 2 * CS), jnp.bfloat16),
        in_specs=[smem, smem, smem, vmem],
        out_specs=vmem,
        cost_estimate=COST,
        name="weights",
    )(role, jnp.asarray(index), jnp.asarray(scale), radial.reshape(20, CS, CS))


def turn_kernel(
    role_ref, field_ref, keep_ref, give_ref, keep_edge_ref, give_edge_ref, give_inner_ref, raw, turned, in_sems, out_sems
):
    odd = role_ref[0] % 2
    loads, stores = [], []
    for p in range(2):
        for q in range(2):
            cells = slice(q * HALF, (q + 1) * HALF)
            copy = pltpu.make_async_copy(
                field_ref.at[(p + odd) % 2, :, cells], raw.at[p, :, cells], in_sems.at[p * 2 + q]
            )
            copy.start()
            loads.append(copy)
    for p in range(2):
        for q in range(2):
            loads[p * 2 + q].wait()
            block = jnp.transpose(raw[p, :, q * HALF : (q + 1) * HALF])
            turned[p, ROW + q * HALF : ROW + (q + 1) * HALF] = block
            if q == 0:
                turned[p, ROW + 2 * HALF :] = block[:ROW]
            if q == 1:
                turned[p, :ROW] = block[-ROW:]
        kept = turned.at[p, pl.ds(pl.multiple_of(odd * HALF, HALF), SLAB)]
        given = turned.at[p, pl.ds(pl.multiple_of((1 - odd) * HALF, HALF), SLAB)]
        wanted = [(given, give_ref.at[p]), (kept, keep_ref.at[p])]
        if p == 0:
            wanted += [(given, give_edge_ref), (kept, keep_edge_ref)]
        else:
            wanted += [(given, give_inner_ref)]
        for source, target in wanted:
            copy = pltpu.make_async_copy(source, target, out_sems.at[len(stores)])
            copy.start()
            stores.append(copy)
    for copy in stores:
        copy.wait()


def turn(role, field):
    single = jax.ShapeDtypeStruct((SLAB, CS), jnp.bfloat16)
    double = jax.ShapeDtypeStruct((2, SLAB, CS), jnp.bfloat16)
    hbm = pl.BlockSpec(memory_space=pl.ANY)
    return pl.pallas_call(
        turn_kernel,
        out_shape=(double, double, single, single, single),
        in_specs=[pl.BlockSpec(memory_space=pltpu.SMEM), hbm],
        out_specs=(hbm,) * 5,
        scratch_shapes=[
            pltpu.VMEM((2, CS, 2 * HALF), jnp.bfloat16),
            pltpu.VMEM((2, 2 * HALF + 2 * ROW, CS), jnp.bfloat16),
            pltpu.SemaphoreType.DMA((4,)),
            pltpu.SemaphoreType.DMA((7,)),
        ],
        compiler_params=pltpu.CompilerParams(vmem_limit_bytes=TURN_VMEM),
        cost_estimate=COST,
        name="turn",
    )(role, field)


def pair_chunk(start, triple, weight, sigma, tau, z_odd):
    def load(ref):
        return ref[start : start + CHUNK + 2 * ROW, :].astype(jnp.float32)

    below, here, above = triple
    if z_odd:
        sources = [load(above) - load(below)]
    else:
        sources = [load(here), load(above) + load(below)]
    features = []
    for source in sources:
        features.append(source[ROW : ROW + CHUNK].astype(jnp.bfloat16))
        features.append((source[2 * ROW :] + sigma * source[:CHUNK]).astype(jnp.bfloat16))
    total = jnp.dot(jnp.concatenate(features, axis=1), weight, preferred_element_type=jnp.float32)
    centre, side = total[:, :CS], total[:, CS:].reshape(CHUNK // ROW, ROW, CS)
    right = pltpu.roll(side, ROW - 1, 1).reshape(CHUNK, CS)
    left = pltpu.roll(side, 1, 1).reshape(CHUNK, CS)
    return centre + right + tau * left


def conv_kernel(jobs, stacks, n_accs, n_outs, role_ref, weight_ref, *refs):
    role = role_ref[0]
    comp, odd = role // 2, role % 2
    gathered = comp ^ (1 + odd)
    reduced = comp ^ (2 - odd)
    pairs = [(comp, comp), (comp, reduced), (gathered, reduced), (gathered, comp)]
    planes = []
    for ref, stack in zip(refs, stacks):
        planes.append([ref] if stack == 0 else [ref.at[at] for at in range(stack)])
    accs = refs[len(stacks) : len(stacks) + n_accs]
    outs = refs[len(refs) - n_outs :]
    if n_outs < len(jobs):
        outs = [*outs[:-1], outs[-1].at[0], outs[-1].at[1]]
    for (triple, slot, acc), out in zip(jobs, outs):
        i, o = pairs[slot]

        def differ(at):
            return (i == at).astype(jnp.int32) != (o == at).astype(jnp.int32)

        tau = jnp.where(differ(1), -1.0, 1.0)
        sigma = jnp.where(differ(2), -1.0, 1.0)
        three = [planes[at][index] for at, index in triple]

        def run(z_odd, rows):
            for start in range(0, HALF, CHUNK):
                value = pair_chunk(start, three, weight_ref[slot, :rows, :], sigma, tau, z_odd)
                if acc is not None:
                    value = value + accs[acc][start : start + CHUNK].astype(jnp.float32)
                out[start : start + CHUNK] = value.astype(out.dtype)

        odd_in_z = differ(3)

        @pl.when(odd_in_z)
        def _():
            run(True, 2 * CS)

        @pl.when(jnp.logical_not(odd_in_z))
        def _():
            run(False, 4 * CS)


def conv(name, role, weight, planes, accs, jobs, types, after=(), cost=COST):
    vmem = pl.BlockSpec(memory_space=pltpu.VMEM)
    stacks = [a.shape[0] if a.ndim == 3 else 0 for a in planes]
    return pl.pallas_call(
        functools.partial(conv_kernel, jobs, stacks, len(accs), len(types)),
        out_shape=tuple(
            jax.ShapeDtypeStruct((2, HALF, CS) if len(types) < len(jobs) and at == len(types) - 1 else (HALF, CS), t)
            for at, t in enumerate(types)
        ),
        in_specs=[pl.BlockSpec(memory_space=pltpu.SMEM)]
        + [vmem] * (1 + len(planes) + len(accs))
        + [pl.BlockSpec(memory_space=pl.ANY)] * len(after),
        out_specs=tuple(vmem for _ in types),
        compiler_params=pltpu.CompilerParams(vmem_limit_bytes=40 << 20),
        cost_estimate=cost,
        name=name,
    )(role, weight, *planes, *accs, *after)


def final_kernel(parts, role_ref, *refs):
    out_ref = refs[-1]
    for p in range(parts):

        @pl.when(pl.program_id(0) == p)
        def _():
            total = refs[p][...].astype(jnp.float32) + refs[parts + p][...].astype(jnp.float32)
            out_ref[0] = jnp.transpose(total.astype(out_ref.dtype))


def final(name, role, places, kept, got, out=None):
    def at(part, role):
        odd = role[0] % 2
        plane, side = (sum(jnp.where(part == p, place[d], 0) for p, place in enumerate(places)) for d in (0, 1))
        return ((plane + odd) % 2, 0, (side + odd) % 2)

    def whole(value):
        if isinstance(value, tuple):
            array, index = value
            return array, pl.BlockSpec((None, HALF, CS), lambda p, role, index=index: (index, 0, 0))
        return value, pl.BlockSpec((HALF, CS), lambda p, role: (0, 0))

    arrays, specs = zip(*[whole(value) for value in (*kept, *got)])
    if out is not None:
        arrays, specs = (*arrays, out), (*specs, pl.BlockSpec(memory_space=pl.ANY))
    return pl.pallas_call(
        functools.partial(final_kernel, len(places)),
        out_shape=jax.ShapeDtypeStruct((2, CS, 2 * HALF), jnp.bfloat16),
        grid_spec=pltpu.PrefetchScalarGridSpec(
            num_scalar_prefetch=1, grid=(len(places),), in_specs=list(specs), out_specs=pl.BlockSpec((1, CS, HALF), at)
        ),
        input_output_aliases={} if out is None else {len(arrays): 0},
        compiler_params=pltpu.CompilerParams(vmem_limit_bytes=40 << 20),
        cost_estimate=COST,
        name=name,
    )(role, *arrays)


def shards(tensor_field, radial):
    n_space, n_chan = lax.axis_size("space"), lax.axis_size("chan")
    sub = n_chan // 4
    chips = n_space // 2
    field = tensor_field
    if sub > 1:
        groups = [[g * sub + h for h in range(sub)] for g in range(4)]
        field = lax.all_gather(field, "chan", axis_index_groups=groups, axis=1, tiled=True)

    def permute(value, place):
        pairs = []
        for s in range(n_space):
            for c in range(4):
                to_s, to_c = place(s // 2, s % 2, c)
                for h in range(sub):
                    pairs.append((s * n_chan + c * sub + h, to_s * n_chan + to_c * sub + h))
        return lax.ppermute(value, ("space", "chan"), pairs)

    def outward(z, k):
        return (z + (1 if k else -1)) % chips

    def gather_group(k, c):
        return c ^ (2 if k else 1)

    def reduce_group(k, c):
        return c ^ (1 if k else 2)

    role = ((lax.axis_index("chan") // sub) * 2 + lax.axis_index("space") % 2).astype(jnp.int32).reshape(1)

    def reduce_near(value):
        return permute(value, lambda z, k, c: (2 * z + k, reduce_group(k, c)))

    def reduce_far(value):
        return permute(value, lambda z, k, c: (2 * z + 1 - k, reduce_group(k, c)))

    def swap(value):
        return permute(value, lambda z, k, c: (2 * z + 1 - k, c))

    def gather_near(value):
        return permute(value, lambda z, k, c: (2 * z + k, gather_group(k, c)))

    def from_far(value):
        return permute(value, lambda z, k, c: (2 * outward(z, k) + k, c))

    f32, bf16 = jnp.float32, jnp.bfloat16
    def gather_cross(value):
        return permute(value, lambda z, k, c: (2 * z + 1 - k, gather_group(1 - k, c)))

    keep, give, keep_edge, give_edge, give_inner = turn(role, field)
    near = gather_near(keep)
    halo_near = permute(give_edge, lambda z, k, c: (2 * outward(z, k) + 1 - k, c))
    halo_far = from_far(keep_edge)
    others = swap(give)
    weight, give_inner = lax.optimization_barrier((weights(role, radial), give_inner))
    near3 = gather_cross(give_inner)

    own_inner = {1: (0, 0), 2: (0, 1), 4: (1, 0), 3: (1, 1)}
    own_all = own_inner | {0: (2, 0), 5: (3, 0)}
    near_all = {1: (0, 0), 2: (0, 1), 3: (1, 0), 4: (2, 0), 0: (3, 0), 5: (4, 0)}

    def jobs(of, *wanted):
        return [(tuple(of[at] for at in (plane - 1, plane, plane + 1)), slot, acc) for plane, slot, acc in wanted]

    own = [keep, others]
    kept2, kept3, lent2, lent3 = conv(
        "own_inner", role, weight, own, [],
        jobs(own_inner, (2, 0, None), (3, 0, None), (2, 1, None), (3, 1, None)), [f32] * 4,
    )
    kept2, near, give_edge = lax.optimization_barrier((kept2, near, give_edge))
    near4 = gather_cross(give_edge)
    far_halo = from_far(near[0])
    sent2, = conv(
        "sent_2", role, weight, [near, near3], [lent2], jobs(near_all, (2, 2, 0)), [bf16], cost=LONG,
    )
    got2 = reduce_near(sent2)
    near_halo = gather_near(halo_near)
    near = [near, near3, near4]
    sent3, = conv(
        "sent_3", role, weight, near, [lent3], jobs(near_all, (3, 2, 0)), [bf16], after=[sent2],
    )
    got3 = reduce_far(sent3)
    kept1, kept4, lent1, lent4 = conv(
        "own_boundary", role, weight, [*own, halo_near, halo_far], [],
        jobs(own_all, (1, 0, None), (4, 0, None), (1, 1, None), (4, 1, None)), [f32] * 4, after=[sent3],
    )
    near = [*near, near_halo, far_halo]
    sent1, = conv(
        "sent_near", role, weight, near[:4], [lent1], jobs(near_all, (1, 2, 0)), [bf16],
    )
    sent4, = conv(
        "sent_far", role, weight, near, [lent4], jobs(near_all, (4, 2, 0)), [bf16], after=[sent1],
    )
    total, = conv(
        "kept_far", role, weight, near, [kept4, kept3],
        jobs(near_all, (4, 3, 0), (3, 3, 1)), [bf16], after=[sent4],
    )
    got1, got4, crossed = reduce_near(sent1), reduce_far(sent4), swap(total)
    total1, total2 = conv(
        "kept_near", role, weight, near, [kept1, kept2],
        jobs(near_all, (1, 3, 0), (2, 3, 1)), [f32] * 2, after=[sent1, got2, got3], cost=LONG,
    )
    out = final(
        "final", role, [(0, 0), (1, 0), (1, 1)], [total1, total2, (crossed, 1)], [got1, got2, got3]
    )
    out = final("final_edge", role, [(0, 1)], [(crossed, 0)], [got4], out)
    if sub > 1:
        out = lax.dynamic_slice_in_dim(out, lax.axis_index("chan") % sub * tensor_field.shape[1], tensor_field.shape[1], 1)
    return out


def solution(mesh):
    placed = (P("space", "chan", None), P())
    return jax.shard_map(
        shards, mesh=mesh, in_specs=placed, out_specs=P("space", "chan", None), check_vma=False
    )
```

```python
import functools

import jax
import jax.numpy as jnp
import numpy as np
from jax import lax
from jax.experimental import pallas as pl
from jax.experimental.pallas import tpu as pltpu
from jax.sharding import PartitionSpec as P


CS = 128
LANES = 128
HALF = 2048
ROW = 64
SLAB = HALF + 2 * ROW
CHUNK = 512
TURN_VMEM = 60 << 20
COST = pl.CostEstimate(flops=1000, bytes_accessed=1000, transcendentals=0)
LONG = pl.CostEstimate(flops=20 * 10**9, bytes_accessed=64 << 20, transcendentals=0)


def weight_tables():
    index = np.zeros((8, 4, 8, 2), np.int32)
    scale = np.zeros((8, 4, 8, 2), np.float32)
    for comp in range(4):
        for odd in range(2):
            gathered = comp ^ (2 if odd else 1)
            reduced = comp ^ (1 if odd else 2)
            pairs = [(comp, comp), (comp, reduced), (gathered, reduced), (gathered, comp)]
            for slot, (i, o) in enumerate(pairs):
                z_odd = (i == 3) != (o == 3)
                for t in range(2):
                    for f in range(4):
                        if z_odd and f >= 2:
                            continue
                        d = (t, f % 2, 1 if (z_odd or f >= 2) else 0)
                        s = sum(d)
                        u = np.float32(np.array(d) / np.sqrt(max(s, 1)))
                        sign = np.float32(-1.0 if (z_odd and odd) else 1.0)
                        kind, first, second = 0, np.float32(0.0), np.float32(0.0)
                        if i == 0 and o == 0:
                            kind, first = 0, np.float32(1.0)
                        elif i == 0:
                            kind, first = 2, u[o - 1]
                        elif o == 0:
                            kind, first = 3, u[i - 1]
                        else:
                            kind = 1
                            first = np.float32(1.0 if i == o else 0.0)
                            second = u[i - 1] * u[o - 1]
                        index[comp * 2 + odd, slot, t * 4 + f] = (kind * 4 + s, 16 + s)
                        scale[comp * 2 + odd, slot, t * 4 + f] = (sign * first, sign * second)
    return index.reshape(8, 64), scale.reshape(8, 64)


def weights_kernel(role_ref, index_ref, scale_ref, radial_ref, out_ref):
    role = role_ref[0]
    for slot in range(4):
        for t in range(2):
            for f in range(4):
                at = (slot * 8 + t * 4 + f) * 2
                first = radial_ref[index_ref[role, at]].astype(jnp.float32) * scale_ref[role, at]
                second = radial_ref[index_ref[role, at + 1]].astype(jnp.float32) * scale_ref[role, at + 1]
                out_ref[slot, f * CS : (f + 1) * CS, t * CS : (t + 1) * CS] = (first + second).astype(jnp.bfloat16)


def weights(role, radial):
    index, scale = weight_tables()
    smem = pl.BlockSpec(memory_space=pltpu.SMEM)
    vmem = pl.BlockSpec(memory_space=pltpu.VMEM)
    return pl.pallas_call(
        weights_kernel,
        out_shape=jax.ShapeDtypeStruct((4, 4 * CS, 2 * CS), jnp.bfloat16),
        in_specs=[smem, smem, smem, vmem],
        out_specs=vmem,
        cost_estimate=COST,
        name="weights",
    )(role, jnp.asarray(index), jnp.asarray(scale), radial.reshape(20, CS, CS))


def turn_kernel(
    role_ref, field_ref, keep_ref, give_ref, keep_edge_ref, give_edge_ref, give_inner_ref, raw, turned, in_sems, out_sems
):
    odd = role_ref[0] % 2
    quarter = HALF // 2
    loads, stores = [], []
    for p in range(2):
        for q in range(4):
            cells = slice(q * quarter, (q + 1) * quarter)
            copy = pltpu.make_async_copy(
                field_ref.at[(p + odd) % 2, :, cells], raw.at[p, :, cells], in_sems.at[p * 4 + q]
            )
            copy.start()
            loads.append(copy)
    for p in range(2):
        for q in range(4):
            loads[p * 4 + q].wait()
            block = jnp.transpose(raw[p, :, q * quarter : (q + 1) * quarter])
            turned[p, ROW + q * quarter : ROW + (q + 1) * quarter] = block
            if q == 0:
                turned[p, ROW + 2 * HALF :] = block[:ROW]
            if q == 3:
                turned[p, :ROW] = block[-ROW:]
        kept = turned.at[p, pl.ds(pl.multiple_of(odd * HALF, HALF), SLAB)]
        given = turned.at[p, pl.ds(pl.multiple_of((1 - odd) * HALF, HALF), SLAB)]
        wanted = [(given, give_ref.at[p]), (kept, keep_ref.at[p])]
        if p == 0:
            wanted += [(given, give_edge_ref), (kept, keep_edge_ref)]
        else:
            wanted += [(given, give_inner_ref)]
        for source, target in wanted:
            copy = pltpu.make_async_copy(source, target, out_sems.at[len(stores)])
            copy.start()
            stores.append(copy)
    for copy in stores:
        copy.wait()


def turn(role, field):
    single = jax.ShapeDtypeStruct((SLAB, CS), jnp.bfloat16)
    double = jax.ShapeDtypeStruct((2, SLAB, CS), jnp.bfloat16)
    hbm = pl.BlockSpec(memory_space=pl.ANY)
    return pl.pallas_call(
        turn_kernel,
        out_shape=(double, double, single, single, single),
        in_specs=[pl.BlockSpec(memory_space=pltpu.SMEM), hbm],
        out_specs=(hbm,) * 5,
        scratch_shapes=[
            pltpu.VMEM((2, CS, 2 * HALF), jnp.bfloat16),
            pltpu.VMEM((2, 2 * HALF + 2 * ROW, CS), jnp.bfloat16),
            pltpu.SemaphoreType.DMA((8,)),
            pltpu.SemaphoreType.DMA((7,)),
        ],
        compiler_params=pltpu.CompilerParams(vmem_limit_bytes=TURN_VMEM),
        cost_estimate=COST,
        name="turn",
    )(role, field)


def pair_chunk(start, triple, weight, sigma, tau, z_odd):
    def load(ref):
        return ref[start : start + CHUNK + 2 * ROW, :].astype(jnp.float32)

    below, here, above = triple
    if z_odd:
        sources = [load(above) - load(below)]
    else:
        sources = [load(here), load(above) + load(below)]
    features = []
    for source in sources:
        features.append(source[ROW : ROW + CHUNK].astype(jnp.bfloat16))
        features.append((source[2 * ROW :] + sigma * source[:CHUNK]).astype(jnp.bfloat16))
    total = jnp.dot(jnp.concatenate(features, axis=1), weight, preferred_element_type=jnp.float32)
    centre, side = total[:, :CS], total[:, CS:].reshape(CHUNK // ROW, ROW, CS)
    right = pltpu.roll(side, ROW - 1, 1).reshape(CHUNK, CS)
    left = pltpu.roll(side, 1, 1).reshape(CHUNK, CS)
    return centre + right + tau * left


def conv_kernel(jobs, stacks, n_accs, n_outs, role_ref, weight_ref, *refs):
    role = role_ref[0]
    comp, odd = role // 2, role % 2
    gathered = comp ^ (1 + odd)
    reduced = comp ^ (2 - odd)
    pairs = [(comp, comp), (comp, reduced), (gathered, reduced), (gathered, comp)]
    planes = []
    for ref, stack in zip(refs, stacks):
        planes.append([ref] if stack == 0 else [ref.at[at] for at in range(stack)])
    accs = refs[len(stacks) : len(stacks) + n_accs]
    outs = refs[len(refs) - n_outs :]
    if n_outs < len(jobs):
        outs = [*outs[:-1], outs[-1].at[0], outs[-1].at[1]]
    for (triple, slot, acc), out in zip(jobs, outs):
        i, o = pairs[slot]

        def differ(at):
            return (i == at).astype(jnp.int32) != (o == at).astype(jnp.int32)

        tau = jnp.where(differ(1), -1.0, 1.0)
        sigma = jnp.where(differ(2), -1.0, 1.0)
        three = [planes[at][index] for at, index in triple]

        def run(z_odd, rows):
            for start in range(0, HALF, CHUNK):
                value = pair_chunk(start, three, weight_ref[slot, :rows, :], sigma, tau, z_odd)
                if acc is not None:
                    value = value + accs[acc][start : start + CHUNK].astype(jnp.float32)
                out[start : start + CHUNK] = value.astype(out.dtype)

        odd_in_z = differ(3)

        @pl.when(odd_in_z)
        def _():
            run(True, 2 * CS)

        @pl.when(jnp.logical_not(odd_in_z))
        def _():
            run(False, 4 * CS)


def conv(name, role, weight, planes, accs, jobs, types, after=(), cost=COST):
    vmem = pl.BlockSpec(memory_space=pltpu.VMEM)
    stacks = [a.shape[0] if a.ndim == 3 else 0 for a in planes]
    return pl.pallas_call(
        functools.partial(conv_kernel, jobs, stacks, len(accs), len(types)),
        out_shape=tuple(
            jax.ShapeDtypeStruct((2, HALF, CS) if len(types) < len(jobs) and at == len(types) - 1 else (HALF, CS), t)
            for at, t in enumerate(types)
        ),
        in_specs=[pl.BlockSpec(memory_space=pltpu.SMEM)]
        + [vmem] * (1 + len(planes) + len(accs))
        + [pl.BlockSpec(memory_space=pl.ANY)] * len(after),
        out_specs=tuple(vmem for _ in types),
        compiler_params=pltpu.CompilerParams(vmem_limit_bytes=40 << 20),
        cost_estimate=cost,
        name=name,
    )(role, weight, *planes, *accs, *after)


def final_kernel(parts, role_ref, *refs):
    out_ref = refs[-1]
    for p in range(parts):

        @pl.when(pl.program_id(0) == p)
        def _():
            total = refs[p][...].astype(jnp.float32) + refs[parts + p][...].astype(jnp.float32)
            out_ref[0] = jnp.transpose(total.astype(out_ref.dtype))


def final(name, role, places, kept, got, out=None):
    def at(part, role):
        odd = role[0] % 2
        plane, side = (sum(jnp.where(part == p, place[d], 0) for p, place in enumerate(places)) for d in (0, 1))
        return ((plane + odd) % 2, 0, (side + odd) % 2)

    def whole(value):
        if isinstance(value, tuple):
            array, index = value
            return array, pl.BlockSpec((None, HALF, CS), lambda p, role, index=index: (index, 0, 0))
        return value, pl.BlockSpec((HALF, CS), lambda p, role: (0, 0))

    arrays, specs = zip(*[whole(value) for value in (*kept, *got)])
    if out is not None:
        arrays, specs = (*arrays, out), (*specs, pl.BlockSpec(memory_space=pl.ANY))
    return pl.pallas_call(
        functools.partial(final_kernel, len(places)),
        out_shape=jax.ShapeDtypeStruct((2, CS, 2 * HALF), jnp.bfloat16),
        grid_spec=pltpu.PrefetchScalarGridSpec(
            num_scalar_prefetch=1, grid=(len(places),), in_specs=list(specs), out_specs=pl.BlockSpec((1, CS, HALF), at)
        ),
        input_output_aliases={} if out is None else {len(arrays): 0},
        compiler_params=pltpu.CompilerParams(vmem_limit_bytes=40 << 20),
        cost_estimate=COST,
        name=name,
    )(role, *arrays)


def shards(tensor_field, radial):
    n_space, n_chan = lax.axis_size("space"), lax.axis_size("chan")
    sub = n_chan // 4
    chips = n_space // 2
    field = tensor_field
    if sub > 1:
        groups = [[g * sub + h for h in range(sub)] for g in range(4)]
        field = lax.all_gather(field, "chan", axis_index_groups=groups, axis=1, tiled=True)

    def permute(value, place):
        pairs = []
        for s in range(n_space):
            for c in range(4):
                to_s, to_c = place(s // 2, s % 2, c)
                for h in range(sub):
                    pairs.append((s * n_chan + c * sub + h, to_s * n_chan + to_c * sub + h))
        return lax.ppermute(value, ("space", "chan"), pairs)

    def outward(z, k):
        return (z + (1 if k else -1)) % chips

    def gather_group(k, c):
        return c ^ (2 if k else 1)

    def reduce_group(k, c):
        return c ^ (1 if k else 2)

    role = ((lax.axis_index("chan") // sub) * 2 + lax.axis_index("space") % 2).astype(jnp.int32).reshape(1)

    def reduce_near(value):
        return permute(value, lambda z, k, c: (2 * z + k, reduce_group(k, c)))

    def reduce_far(value):
        return permute(value, lambda z, k, c: (2 * z + 1 - k, reduce_group(k, c)))

    def swap(value):
        return permute(value, lambda z, k, c: (2 * z + 1 - k, c))

    def gather_near(value):
        return permute(value, lambda z, k, c: (2 * z + k, gather_group(k, c)))

    def from_far(value):
        return permute(value, lambda z, k, c: (2 * outward(z, k) + k, c))

    f32, bf16 = jnp.float32, jnp.bfloat16
    def gather_cross(value):
        return permute(value, lambda z, k, c: (2 * z + 1 - k, gather_group(1 - k, c)))

    keep, give, keep_edge, give_edge, give_inner = turn(role, field)
    near = gather_near(keep)
    halo_near = permute(give_edge, lambda z, k, c: (2 * outward(z, k) + 1 - k, c))
    halo_far = from_far(keep_edge)
    others = swap(give)
    weight = weights(role, radial)
    near3 = gather_cross(give_inner)

    own_inner = {1: (0, 0), 2: (0, 1), 4: (1, 0), 3: (1, 1)}
    own_all = own_inner | {0: (2, 0), 5: (3, 0)}
    near_all = {1: (0, 0), 2: (0, 1), 3: (1, 0), 4: (2, 0), 0: (3, 0), 5: (4, 0)}

    def jobs(of, *wanted):
        return [(tuple(of[at] for at in (plane - 1, plane, plane + 1)), slot, acc) for plane, slot, acc in wanted]

    own = [keep, others]
    kept2, kept3, lent2, lent3 = conv(
        "own_inner", role, weight, own, [],
        jobs(own_inner, (2, 0, None), (3, 0, None), (2, 1, None), (3, 1, None)), [f32] * 4,
    )
    kept2, near, give_edge = lax.optimization_barrier((kept2, near, give_edge))
    near4 = gather_cross(give_edge)
    far_halo = from_far(near[0])
    sent2, = conv(
        "sent_2", role, weight, [near, near3], [lent2], jobs(near_all, (2, 2, 0)), [bf16], cost=LONG,
    )
    got2 = reduce_near(sent2)
    near_halo = gather_near(halo_near)
    near = [near, near3, near4]
    sent3, = conv(
        "sent_3", role, weight, near, [lent3], jobs(near_all, (3, 2, 0)), [bf16], after=[sent2],
    )
    got3 = reduce_far(sent3)
    kept1, kept4, lent1, lent4 = conv(
        "own_boundary", role, weight, [*own, halo_near, halo_far], [],
        jobs(own_all, (1, 0, None), (4, 0, None), (1, 1, None), (4, 1, None)), [f32] * 4, after=[sent3],
    )
    near = [*near, near_halo, far_halo]
    sent1, = conv(
        "sent_near", role, weight, near[:4], [lent1], jobs(near_all, (1, 2, 0)), [bf16],
    )
    sent4, total = conv(
        "far", role, weight, near, [lent4, kept4, kept3],
        jobs(near_all, (4, 2, 0), (4, 3, 1), (3, 3, 2)), [bf16] * 2, after=[sent1],
    )
    got1, got4, crossed = reduce_near(sent1), reduce_far(sent4), swap(total)
    total1, total2 = conv(
        "kept_near", role, weight, near, [kept1, kept2],
        jobs(near_all, (1, 3, 0), (2, 3, 1)), [f32] * 2, after=[sent1, got2, got3], cost=LONG,
    )
    out = final(
        "final", role, [(0, 0), (1, 0), (1, 1)], [total1, total2, (crossed, 1)], [got1, got2, got3]
    )
    out = final("final_edge", role, [(0, 1)], [(crossed, 0)], [got4], out)
    if sub > 1:
        out = lax.dynamic_slice_in_dim(out, lax.axis_index("chan") % sub * tensor_field.shape[1], tensor_field.shape[1], 1)
    return out


def solution(mesh):
    placed = (P("space", "chan", None), P())
    return jax.shard_map(
        shards, mesh=mesh, in_specs=placed, out_specs=P("space", "chan", None), check_vma=False
    )
```
